32 devices in a mesh: groups: 2 (over x), seq: 16 (over z, y, core).
Axes of the slice: x: 2, y: 2, z: 4, core: 2. Of those that a mesh axis runs over, the one named last changes fastest.
Arguments:
- queries: bfloat16 [96, 8192], P(('groups', 'seq')), parts along dimension 0, may hold values from -9 to 9, as said below
- key_rows: bfloat16 [8192, 8192], P(('groups', 'seq')), parts along dimension 0, may hold values from -9 to 9, as said below
- value_rows: bfloat16 [8192, 8192], P(('groups', 'seq')), parts along dimension 0, may hold values from -6 to 6
- out_weight: bfloat16 [8192, 4096], P('seq'), may hold values from -6 to 6
- levels: int32 [3, 96], P(None, ('groups', 'seq')), parts along dimension 1, may hold values from 0 to 8
- owner_map: int32 [3, 96], P(None, ('groups', 'seq')), parts along dimension 1, may hold values from 0 to 47, each once within a row
Outputs:
- base_update: bfloat16 [96, 4096], P(('groups', 'seq')), parts along dimension 0
The draws below stay inside these ranges and needn't reach their ends.
There are 2 independent parts, one for each index of `groups`. The reference program is written for one: setup_inputs(seed, part) draws one part's arguments, and reference() takes and returns one part's arrays. A program takes and returns all parts, laid end to end along the dimension named above; an argument that names none is the same for every part. Nothing has to cross between parts.
Inputs may be any that keep to these rules, and one draw needn't show every extreme that they name: queries: of order one, a few entries larger. key_rows: of order one, a few entries larger. Each row of owner_map names every base query token once; it stands in for a resampling onto base positions.
All inputs are finite; a program needn't handle non-finite values.
Results may differ from the reference program's by a relative error of at most 0.02.
Values may be sent and summed in bfloat16 or wider, within the bound.
No kernel may reach another device: no remote copies, remote signals or barrier semaphores. Data moves between devices by JAX's collectives and lax.ppermute only.
A program may use at most 128 MiB of HBM per device.

```python
import jax
import jax.numpy as jnp
from jax import lax

D = 4096
HD = 128
HEADS = 16
SECTIONS = 4
CONTROLS = 3
LEVELS = 8
QUERIES = 48
KEYS = 4096


def draw_queries(key, part):
    shape = (QUERIES, SECTIONS * HEADS * HD)
    base = jnp.clip(jax.random.normal(jax.random.fold_in(key, 1), shape, jnp.float32), -6.0, 6.0)
    return base.astype(jnp.bfloat16)


def draw_key_rows(key, part):
    shape = (KEYS, SECTIONS * HEADS * HD)
    base = jnp.clip(jax.random.normal(jax.random.fold_in(key, 2), shape, jnp.float32), -6.0, 6.0)
    return base.astype(jnp.bfloat16)


def with_ends(drawn, stream_key, low, top_value):
    spot = [jax.random.randint(jax.random.fold_in(stream_key, axis), (), 0, length) for axis, length in enumerate(drawn.shape)]
    longest = drawn.shape.index(max(drawn.shape))
    neighbour = spot[:longest] + [(spot[longest] + 1) % drawn.shape[longest]] + spot[longest + 1:]
    return drawn.at[tuple(spot)].set(low).at[tuple(neighbour)].set(top_value)


def steps_of(own_key, dims, shards, low, high):
    level, own = 1.0, jax.random.fold_in(own_key, 6)
    for dim, blocks in shards:
        heights = jnp.exp(jax.random.uniform(jax.random.fold_in(own, dim), (blocks,), jnp.float32, low / len(shards), high / len(shards)))
        level = level * jnp.repeat(heights, dims[dim] // blocks).reshape([-1 if axis == dim else 1 for axis in range(len(dims))])
    return level


def gaussian(stream_key, shape, spread, most, cuts=(), dtype=jnp.bfloat16):
    factor_of = steps_of(stream_key, shape, cuts, -0.22, 0.18) if cuts else 1.0
    values = jax.random.normal(stream_key, shape, jnp.float32) * spread * factor_of
    return jnp.minimum(jnp.maximum(values, -most), most).astype(dtype)


def setup_inputs(seed: int = 0, part: int = 0) -> dict:
    keys = jax.random.split(jax.random.key(seed), 7)
    own_keys = jax.random.split(jax.random.fold_in(keys[6], part), 7)
    return {
        "queries": draw_queries(jax.random.fold_in(jax.random.fold_in(keys[6], part), 71), part),
        "key_rows": draw_key_rows(jax.random.fold_in(jax.random.fold_in(keys[6], part), 71), part),
        "value_rows": gaussian(own_keys[2], (KEYS, SECTIONS * HEADS * HD), 1.0, 6.0, ((0, 16),)),
        "out_weight": gaussian(keys[3], (SECTIONS * HEADS * HD, D), 1.0, 6.0, ((0, 16),)),
        "levels": with_ends(jax.random.randint(own_keys[4], (CONTROLS, QUERIES), 0, LEVELS + 1), jax.random.fold_in(own_keys[4], 1), 0, LEVELS).astype(jnp.int32),
        "owner_map": jax.vmap(lambda own: jax.random.permutation(own, QUERIES))(jax.random.split(own_keys[5], CONTROLS)).reshape((CONTROLS, QUERIES)).astype(jnp.int32),
    }


def attend(operands):
    query_head, key_head, value_head = operands
    scores = jnp.dot(query_head, key_head.T, preferred_element_type=jnp.float32) * (HD ** -0.5)
    peak = jnp.max(scores, axis=1)
    expo = jnp.exp(scores - peak[:, None])
    total = jnp.sum(expo, axis=1)
    weighted = jnp.dot(expo.astype(jnp.bfloat16), value_head, preferred_element_type=jnp.float32)
    return (weighted / total[:, None]).astype(jnp.bfloat16)


def reference(queries, key_rows, value_rows, out_weight, levels, owner_map):
    pairs = SECTIONS * HEADS
    query_heads = queries.reshape(QUERIES, pairs, HD).transpose(1, 0, 2)
    key_heads = key_rows.reshape(KEYS, pairs, HD).transpose(1, 0, 2)
    value_heads = value_rows.reshape(KEYS, pairs, HD).transpose(1, 0, 2)
    attended = lax.map(attend, (query_heads, key_heads, value_heads))
    result = jnp.zeros((QUERIES, D), jnp.float32)
    for section in range(SECTIONS):
        block = attended[section * HEADS:(section + 1) * HEADS].transpose(1, 0, 2).reshape(QUERIES, HEADS * HD)
        weight_rows = out_weight[section * HEADS * HD:(section + 1) * HEADS * HD]
        projected = jnp.dot(block, weight_rows, preferred_element_type=jnp.float32)
        if section < CONTROLS:
            factor = levels[section].astype(jnp.float32) / LEVELS
            result = result.at[owner_map[section]].add(projected * factor[:, None])
        else:
            result = result + projected
    return result.astype(jnp.bfloat16)
```

```python
import functools

import jax
import jax.numpy as jnp
from jax import lax
from jax.experimental import pallas as pl
from jax.experimental.pallas import tpu as pltpu
from jax.sharding import PartitionSpec as P

HD = 128
HEADS = 16
CONTROLS = 3
LEVELS = 8
LANES = 128
BASE = 256

VMEM = pl.BlockSpec(memory_space=pltpu.VMEM)


def rows_of(tokens, heads_dev):
    tiles = -(-tokens // LANES)
    return heads_dev * tokens, tiles, -(-(2 * heads_dev * tiles) // 8) * 8


def attend_kernel(tokens, heads_dev, q_ref, k_ref, v_ref, out_ref, stat_ref):
    pairs = k_ref.shape[1] // HD
    main, tiles, _ = rows_of(tokens, heads_dev)
    group = max(4, heads_dev)
    lane = lax.broadcasted_iota(jnp.int32, (tokens, LANES), 1)
    stat_ref[...] = jnp.zeros_like(stat_ref)

    def step(g, carry):
        stat = stat_ref[:tokens, :]
        for first in range(0, group, 2):
            expo = []
            for j in (first, first + 1):
                head = g * group + j
                columns = pl.ds(pl.multiple_of(head * HD, HD), HD)
                scores = lax.dot_general(
                    q_ref[:, columns], k_ref[:, columns], (((1,), (1,)), ((), ())), preferred_element_type=jnp.float32
                ) * HD ** (-0.5)
                peak = jnp.max(scores, axis=1, keepdims=True).astype(jnp.bfloat16).astype(jnp.float32)
                weights = jnp.exp(scores - peak)
                total = jnp.sum(weights, axis=1, keepdims=True)
                expo.append(weights.astype(jnp.bfloat16))
                place = (g * (group // heads_dev) + j // heads_dev) * 2 * heads_dev + j % heads_dev
                stat = jnp.where(lane == place, peak, jnp.where(lane == place + heads_dev, total, stat))
            both = pl.ds(pl.multiple_of((g * group + first) * HD, 2 * HD), 2 * HD)
            product = jnp.dot(jnp.concatenate(expo, axis=0), v_ref[:, both], preferred_element_type=jnp.float32)
            for i, j in enumerate((first, first + 1)):
                row = (j % heads_dev) * tokens
                out_ref[g * (group // heads_dev) + j // heads_dev, row : row + tokens, :] = product[
                    i * tokens : (i + 1) * tokens, i * HD : (i + 1) * HD
                ].astype(jnp.bfloat16)
        stat_ref[:tokens, :] = stat
        return carry

    lax.fori_loop(0, pairs // group, step, 0, unroll=2)
    for tile in range(tiles):
        turned = stat_ref[tile * LANES : (tile + 1) * LANES, :].T.astype(jnp.bfloat16)
        for device in range(pairs // heads_dev):
            at = main + tile * 2 * heads_dev
            out_ref[device, at : at + 2 * heads_dev, :] = turned[device * 2 * heads_dev : (device + 1) * 2 * heads_dev, :]


def project_kernel(tokens, heads_dev, x_ref, w_ref, meta_ref, out_ref):
    count = x_ref.shape[0]
    main, tiles, _ = rows_of(tokens, heads_dev)
    span = 2 * heads_dev
    shares = []
    for tile in range(tiles):
        at = main + tile * span
        rows = jnp.concatenate([x_ref[i, at : at + span, :].astype(jnp.float32) for i in range(count)], axis=0)
        stat = rows.T
        best, shift = stat, span
        while shift < LANES:
            best = jnp.maximum(best, pltpu.roll(best, shift, 1))
            shift *= 2
        factor = jnp.exp(stat - best)
        denom, shift = factor * pltpu.roll(stat, LANES - heads_dev, 1), span
        while shift < LANES:
            denom = denom + pltpu.roll(denom, shift, 1)
            shift *= 2
        shares.append(factor / denom)
    share = jnp.concatenate(shares, axis=0)[:tokens, :]
    attended = []
    for h in range(heads_dev):
        total = jnp.zeros((tokens, HD), jnp.float32)
        for i in range(count):
            part = x_ref[i, h * tokens : (h + 1) * tokens, :].astype(jnp.float32)
            total = total + share[:, i * span + h : i * span + h + 1] * part
        attended.append(total.astype(jnp.bfloat16))
    attended = jnp.concatenate(attended, axis=1)

    section = lax.axis_index("seq") * heads_dev // HEADS
    control = jnp.minimum(section, CONTROLS - 1)
    is_base = section >= CONTROLS
    meta = meta_ref[...].astype(jnp.float32)
    lane = lax.broadcasted_iota(jnp.int32, meta.shape, 1)

    def column(index):
        return jnp.sum(jnp.where(lane == index, meta, 0.0), axis=1, keepdims=True)

    owner = column(CONTROLS + control) + BASE * column(2 * CONTROLS + control)
    level = column(control)
    token = lax.broadcasted_iota(jnp.int32, (tokens, 1), 0).astype(jnp.float32)
    owner = jnp.where(is_base, token, owner)
    level = jnp.where(is_base, float(LEVELS), level)
    places = lax.broadcasted_iota(jnp.int32, (tokens, tokens), 1).astype(jnp.float32)
    selector = (owner == places).astype(jnp.bfloat16)
    turn = (((0,), (0,)), ((), ()))
    mixed = lax.dot_general(selector, attended, turn, preferred_element_type=jnp.float32).astype(jnp.bfloat16)
    wide = jnp.broadcast_to(level, (tokens, LANES)).astype(jnp.bfloat16)
    weight = lax.dot_general(selector, wide, turn, preferred_element_type=jnp.float32)[:, :1] / LEVELS
    width = 512
    for at in range(0, w_ref.shape[1], width):
        out_ref[:, at : at + width] = (
            jnp.dot(mixed, w_ref[:, at : at + width], preferred_element_type=jnp.float32) * weight
        ).astype(jnp.bfloat16)


def on_device(queries, key_rows, value_rows, out_weight, levels, owner_map):
    count = lax.axis_size("seq")
    tokens = queries.shape[0] * count
    pairs = queries.shape[1] // HD
    heads_dev = out_weight.shape[0] // HD
    main, tiles, extra = rows_of(tokens, heads_dev)
    meta = jnp.concatenate([levels, owner_map % BASE, owner_map // BASE], axis=0).T.astype(jnp.bfloat16)
    meta = jnp.pad(meta, ((0, 0), (0, LANES - meta.shape[1])))
    gathered = lax.all_gather(jnp.concatenate([queries, meta], axis=1), "seq", axis=0, tiled=True)
    parts = pl.pallas_call(
        functools.partial(attend_kernel, tokens, heads_dev),
        out_shape=jax.ShapeDtypeStruct((count, main + extra, HD), jnp.bfloat16),
        in_specs=[VMEM] * 3,
        out_specs=VMEM,
        scratch_shapes=[pltpu.VMEM((tiles * LANES, LANES), jnp.float32)],
        name="attend",
    )(gathered, key_rows, value_rows)
    parts = lax.all_to_all(parts, "seq", split_axis=0, concat_axis=0, tiled=True)
    projected = pl.pallas_call(
        functools.partial(project_kernel, tokens, heads_dev),
        out_shape=jax.ShapeDtypeStruct((tokens, out_weight.shape[1]), jnp.bfloat16),
        in_specs=[VMEM] * 3,
        out_specs=VMEM,
        name="project",
    )(parts, out_weight, gathered[:, pairs * HD :])
    summed = lax.all_to_all(
        projected.reshape(count, tokens // count, -1), "seq", split_axis=0, concat_axis=0, tiled=True
    )
    return jnp.sum(summed.astype(jnp.float32), axis=0).astype(jnp.bfloat16)


def solution(mesh):
    return jax.shard_map(
        on_device,
        mesh=mesh,
        in_specs=(
            P(("groups", "seq"), None),
            P(("groups", "seq"), None),
            P(("groups", "seq"), None),
            P("seq", None),
            P(None, ("groups", "seq")),
            P(None, ("groups", "seq")),
        ),
        out_specs=P(("groups", "seq"), None),
        check_vma=False,
    )
```

```python
import functools

import jax
import jax.numpy as jnp
from jax import lax
from jax.experimental import pallas as pl
from jax.experimental.pallas import tpu as pltpu
from jax.sharding import PartitionSpec as P

HD = 128
HEADS = 16
CONTROLS = 3
LEVELS = 8
LANES = 128
BASE = 256
TO_EXP2 = HD ** (-0.5) * 1.4426950408889634


VMEM = pl.BlockSpec(memory_space=pltpu.VMEM)
SMEM = pl.BlockSpec(memory_space=pltpu.SMEM)
ANY = pl.BlockSpec(memory_space=pl.ANY)


def tiles_of(tokens):
    return -(-tokens // LANES)


def pack_kernel(width, q_ref, level_ref, owner_ref, mine_ref, other_ref):
    core = lax.rem(lax.axis_index("seq"), 2)
    rows, chips = q_ref.shape[0], q_ref.shape[1] // (2 * width)
    row = lax.broadcasted_iota(jnp.int32, (mine_ref.shape[0], LANES), 0)
    lane = lax.broadcasted_iota(jnp.int32, (mine_ref.shape[0], LANES), 1)
    meta = jnp.zeros((mine_ref.shape[0], LANES), jnp.int32)
    for c in range(CONTROLS):
        for t in range(rows):
            owner = owner_ref[c, t]
            for index, value in ((c, level_ref[c, t]), (CONTROLS + c, owner & (BASE - 1)), (2 * CONTROLS + c, owner >> 8)):
                meta = jnp.where((row == t) & (lane == index), value, meta)
    meta = meta.astype(jnp.float32).astype(jnp.bfloat16)
    for parity, ref in ((core, mine_ref), (1 - core, other_ref)):
        ref[...] = jnp.zeros_like(ref)
        for chip in range(chips):
            start = pl.multiple_of((2 * chip + parity) * width, LANES)
            ref[:rows, chip * width : (chip + 1) * width] = q_ref[:, pl.ds(start, width)]
        ref[:, chips * width :] = meta


def attend_kernel(tokens, rows, heads_dev, q_refs, key_refs, value_refs, out_refs, meta_ref, q_ref, k_ref, v_ref, sem, stat_ref):
    me = lax.axis_index("seq")
    core, here = lax.rem(me, 2), me // 2
    chips = len(out_refs)
    width = heads_dev * HD
    keys = key_refs[0].shape[0]
    main = heads_dev * tokens

    def block(d):
        return jnp.bitwise_xor(here, d)

    def copies(d):
        at = pl.ds(pl.multiple_of((2 * block(d) + core) * width, LANES), width)
        to = pl.ds(d * width, width)
        for s, refs, buffer in ((0, key_refs, k_ref), (1, value_refs, v_ref)):
            for i, ref in enumerate(refs):
                yield pltpu.make_async_copy(ref.at[:, at], buffer.at[i * keys : (i + 1) * keys, to], sem.at[s, i, d])

    for d in range(chips):
        for copy in copies(d):
            copy.start()

    slots = q_refs[0].shape[0] // 2
    total = 0.0
    token = lax.broadcasted_iota(jnp.int32, (tokens, q_refs[0].shape[0]), 0)
    slot = lax.broadcasted_iota(jnp.int32, (tokens, q_refs[0].shape[0]), 1)
    part = slot % 8
    j = part % 4
    for low, ref in enumerate(q_refs):
        source = jnp.bitwise_xor(here, 2 * (slot // 8) + low)
        place = (2 * source + jnp.bitwise_xor(core, part // 4)) * rows + j
        pick = ((place == token) & (j < rows)).astype(jnp.bfloat16)
        total = total + jnp.dot(pick, ref[...], preferred_element_type=jnp.float32)
    total = total.astype(jnp.bfloat16)
    q_ref[...] = total[:, : chips * width]
    meta_ref[...] = total[:, chips * width :]

    lane = lax.broadcasted_iota(jnp.int32, (tokens, LANES), 1)
    stat_ref[...] = jnp.zeros_like(stat_ref)
    stat = jnp.zeros((tokens, LANES), jnp.float32)
    group = 8
    heads = [(d, h) for d in range(chips) for h in range(heads_dev)]
    for first in range(0, len(heads), group):
        some = heads[first : first + group]
        for d in sorted({d for d, _ in some}):
            for copy in copies(d):
                copy.wait()
        scores = []
        for d, h in some:
            columns = slice(d * width + h * HD, d * width + (h + 1) * HD)
            query = q_ref[:, pl.ds(pl.multiple_of(block(d) * width + h * HD, LANES), HD)]
            scores.append(
                lax.dot_general(query, k_ref[:, columns], (((1,), (1,)), ((), ())), preferred_element_type=jnp.float32)
            )
        expo = []
        for (d, h), score in zip(some, scores):
            peak = jnp.max(score, axis=1, keepdims=True).astype(jnp.bfloat16).astype(jnp.float32)
            weights = jnp.exp2((score - peak) * TO_EXP2)
            rowsum = jnp.sum(weights, axis=1, keepdims=True)
            expo.append(weights.astype(jnp.bfloat16))
            at = d * 2 * heads_dev + h
            stat = jnp.where(lane == at, peak, jnp.where(lane == at + heads_dev, rowsum, stat))
        for i in range(0, len(some), 2):
            columns = slice((first + i) * HD, (first + i + 2) * HD)
            product = jnp.dot(jnp.concatenate(expo[i : i + 2], axis=0), v_ref[:, columns], preferred_element_type=jnp.float32)
            for k in range(2):
                d, h = some[i + k]
                out_refs[d][h * tokens : (h + 1) * tokens, :] = product[
                    k * tokens : (k + 1) * tokens, k * HD : (k + 1) * HD
                ].astype(jnp.bfloat16)
    stat_ref[:tokens, :] = stat
    span = 2 * heads_dev
    for tile in range(tiles_of(tokens)):
        turned = stat_ref[tile * LANES : (tile + 1) * LANES, :].T.astype(jnp.bfloat16)
        for d in range(chips):
            out_refs[d][main + tile * span : main + (tile + 1) * span, :] = turned[d * span : (d + 1) * span, :]


def project_kernel(tokens, rows, heads_dev, x_refs, w_hbm, meta_ref, mine_ref, other_ref, w_ref, sem):
    me = lax.axis_index("seq")
    core = lax.rem(me, 2)
    chips = len(x_refs)
    step = 512
    chunks = w_hbm.shape[1] // step

    def copy(i):
        at = pl.ds(i * step, step)
        return pltpu.make_async_copy(w_hbm.at[:, at], w_ref.at[:, at], sem.at[i])

    for i in range(chunks):
        copy(i).start()

    main, span = heads_dev * tokens, 2 * heads_dev
    shares = []
    for tile in range(tiles_of(tokens)):
        at = main + tile * span
        stat = [x_ref[at : at + span, :].astype(jnp.float32) for x_ref in x_refs]
        stat = jnp.concatenate(stat + [jnp.zeros((LANES - chips * span, LANES), jnp.float32)], axis=0).T
        stat = jnp.where(lax.broadcasted_iota(jnp.int32, stat.shape, 1) < chips * span, stat, -1e30)
        best, shift = stat, span
        while shift < LANES:
            best = jnp.maximum(best, pltpu.roll(best, shift, 1))
            shift *= 2
        factor = jnp.exp2((stat - best) * TO_EXP2)
        denom, shift = factor * pltpu.roll(stat, LANES - heads_dev, 1), span
        while shift < LANES:
            denom = denom + pltpu.roll(denom, shift, 1)
            shift *= 2
        shares.append(factor / denom)
    share = jnp.concatenate(shares, axis=0)[:tokens, :]
    attended = []
    for h in range(heads_dev):
        total = jnp.zeros((tokens, HD), jnp.float32)
        for i, x_ref in enumerate(x_refs):
            at = i * span + h
            total = total + share[:, at : at + 1] * x_ref[h * tokens : (h + 1) * tokens, :].astype(jnp.float32)
        attended.append(total.astype(jnp.bfloat16))
    attended = jnp.concatenate(attended, axis=1)

    section = me * heads_dev // HEADS
    control = jnp.minimum(section, CONTROLS - 1)
    is_base = section >= CONTROLS
    meta = meta_ref[...].astype(jnp.float32)
    lane = lax.broadcasted_iota(jnp.int32, meta.shape, 1)

    def column(index):
        return jnp.sum(jnp.where(lane == index, meta, 0.0), axis=1, keepdims=True)

    token = lax.broadcasted_iota(jnp.int32, (tokens, 1), 0)
    owner = column(CONTROLS + control) + BASE * column(2 * CONTROLS + control)
    owner = jnp.where(is_base, token, owner.astype(jnp.int32))
    level = jnp.where(is_base, float(LEVELS), column(control))
    out = lax.broadcasted_iota(jnp.int32, (tokens, 2 * chips * 8), 1)
    j = out % 8
    chip = (out // 8) % chips
    parity = jnp.bitwise_xor(core, out // (8 * chips))
    base = jnp.where(j < rows, (2 * chip + parity) * rows + j, -1)
    selector = (owner == base).astype(jnp.bfloat16)
    turn = (((0,), (0,)), ((), ()))
    mixed = lax.dot_general(selector, attended, turn, preferred_element_type=jnp.float32).astype(jnp.bfloat16)
    wide = jnp.broadcast_to(level, (tokens, LANES)).astype(jnp.bfloat16)
    weight = lax.dot_general(selector, wide, turn, preferred_element_type=jnp.float32)[:, :1] / LEVELS
    for i in range(chunks):
        copy(i).wait()
        at = slice(i * step, (i + 1) * step)
        product = jnp.dot(mixed, w_ref[:, at], preferred_element_type=jnp.float32) * weight
        for c in range(chips):
            mine_ref[c, :, at] = product[8 * c : 8 * c + rows, :]
            other_ref[c, :, at] = product[8 * (chips + c) : 8 * (chips + c) + rows, :].astype(jnp.bfloat16)


def call(kernel, splits, out_shape, in_specs, scratch, name, args):
    def body(*refs):
        grouped, at = [], 0
        for size in splits:
            grouped.append(refs[at] if size == 0 else refs[at : at + size])
            at += max(size, 1)
        kernel(*grouped, *refs[at:])

    return pl.pallas_call(
        body,
        out_shape=out_shape,
        in_specs=in_specs,
        out_specs=jax.tree.map(lambda _: VMEM, out_shape),
        scratch_shapes=scratch,
        name=name,
    )(*args)


def on_device(queries, key_rows, value_rows, out_weight, levels, owner_map):
    count = lax.axis_size("seq")
    chips, rows = count // 2, queries.shape[0]
    tokens = rows * count
    heads_dev = out_weight.shape[0] // HD
    width = heads_dev * HD
    keys = key_rows.shape[0]
    extra = -(-2 * heads_dev * tiles_of(tokens) // 8) * 8

    def swap(x, bits):
        return lax.ppermute(x, "seq", [(i, i ^ bits) for i in range(count)])

    packed = jax.ShapeDtypeStruct((4, chips * width + LANES), jnp.bfloat16)
    mine, other = call(
        functools.partial(pack_kernel, width), (0, 0, 0), [packed, packed], [VMEM, SMEM, SMEM], [], "pack",
        (queries, levels, owner_map),
    )
    mine = jnp.concatenate([mine, swap(other, 1)], axis=0)
    mine = jnp.concatenate([mine] + [swap(mine, 2 * d) for d in range(2, chips, 2)], axis=0)
    near = swap(mine, 2)
    key_there, value_there = swap(key_rows, 1), swap(value_rows, 1)

    part = jax.ShapeDtypeStruct((heads_dev * tokens + extra, HD), jnp.bfloat16)
    *parts, meta = call(
        functools.partial(attend_kernel, tokens, rows, heads_dev),
        (2, 2, 2, chips),
        [part] * chips + [jax.ShapeDtypeStruct((tokens, LANES), jnp.bfloat16)],
        [VMEM] * 2 + [ANY] * 4,
        [
            pltpu.VMEM((tokens, chips * width), jnp.bfloat16),
            pltpu.VMEM((2 * keys, chips * width), jnp.bfloat16),
            pltpu.VMEM((2 * keys, chips * width), jnp.bfloat16),
            pltpu.SemaphoreType.DMA((2, 2, chips)),
            pltpu.VMEM((tiles_of(tokens) * LANES, LANES), jnp.float32),
        ],
        "attend",
        (mine, near, key_rows, key_there, value_rows, value_there),
    )
    parts = parts[:1] + [swap(parts[d], 2 * d) for d in range(1, chips)]
    share = (chips, rows, out_weight.shape[1])
    mine, other = call(
        functools.partial(project_kernel, tokens, rows, heads_dev),
        (chips,),
        [jax.ShapeDtypeStruct(share, jnp.float32), jax.ShapeDtypeStruct(share, jnp.bfloat16)],
        [VMEM] * chips + [ANY, VMEM],
        [pltpu.VMEM(out_weight.shape, out_weight.dtype), pltpu.SemaphoreType.DMA((out_weight.shape[1] // 512,))],
        "project",
        (*parts, out_weight, meta),
    )
    summed = (mine + swap(other, 1).astype(jnp.float32)).astype(jnp.bfloat16)
    groups = [list(range(c, count, 2)) for c in range(2)]
    summed = lax.all_to_all(summed, "seq", split_axis=0, concat_axis=0, axis_index_groups=groups, tiled=True)
    return jnp.sum(summed.astype(jnp.float32), axis=0).astype(jnp.bfloat16)


def solution(mesh):
    return jax.shard_map(
        on_device,
        mesh=mesh,
        in_specs=(
            P(("groups", "seq"), None),
            P(("groups", "seq"), None),
            P(("groups", "seq"), None),
            P("seq", None),
            P(None, ("groups", "seq")),
            P(None, ("groups", "seq")),
        ),
        out_specs=P(("groups", "seq"), None),
        check_vma=False,
    )
```

```python
import functools

import jax
import jax.numpy as jnp
from jax import lax
from jax.experimental import pallas as pl
from jax.experimental.pallas import tpu as pltpu
from jax.sharding import PartitionSpec as P

HD = 128
HEADS = 16
CONTROLS = 3
LEVELS = 8
LANES = 128
BASE = 256
TO_EXP2 = HD ** (-0.5) * 1.4426950408889634


VMEM = pl.BlockSpec(memory_space=pltpu.VMEM)
SMEM = pl.BlockSpec(memory_space=pltpu.SMEM)
IN_HBM = pl.BlockSpec(memory_space=pltpu.HBM)


def tiles_of(tokens):
    return -(-tokens // LANES)


def pack_kernel(width, here_refs, there_refs, out_ref):
    core = lax.rem(lax.axis_index("seq"), 2)
    q_ref = here_refs[0]
    rows, chips = q_ref.shape[0], q_ref.shape[1] // (2 * width)
    row = lax.broadcasted_iota(jnp.int32, (8, LANES), 0)
    lane = lax.broadcasted_iota(jnp.int32, (8, LANES), 1)
    meta = jnp.zeros((8, LANES), jnp.int32)
    out_ref[...] = jnp.zeros_like(out_ref)
    for i, (q_ref, level_ref, owner_ref) in enumerate((here_refs, there_refs)):
        for c in range(CONTROLS):
            for t in range(rows):
                owner = owner_ref[c, t]
                for index, value in (
                    (c, level_ref[c, t]), (CONTROLS + c, owner & (BASE - 1)), (2 * CONTROLS + c, owner >> 8)
                ):
                    meta = jnp.where((row == 4 * i + t) & (lane == index), value, meta)
        for chip in range(chips):
            start = pl.multiple_of((2 * chip + core) * width, LANES)
            out_ref[4 * i : 4 * i + rows, chip * width : (chip + 1) * width] = q_ref[:, pl.ds(start, width)]
    out_ref[:, chips * width :] = meta.astype(jnp.float32).astype(jnp.bfloat16)


def attend_kernel(tokens, rows, heads_dev, q_refs, key_refs, value_refs, out_ref, meta_ref, q_ref, k_ref, v_ref, sem, stat_ref):
    me = lax.axis_index("seq")
    core, here = lax.rem(me, 2), me // 2
    chips = len(q_refs)
    width = heads_dev * HD
    keys = key_refs[0].shape[0]
    main = heads_dev * tokens

    def block(d):
        return jnp.bitwise_xor(here, d)

    def copies(d):
        at = pl.ds(pl.multiple_of((2 * block(d) + core) * width, LANES), width)
        to = pl.ds(d * width, width)
        for s, refs, buffer in ((0, key_refs, k_ref), (1, value_refs, v_ref)):
            for i, ref in enumerate(refs):
                yield pltpu.make_async_copy(ref.at[:, at], buffer.at[i * keys : (i + 1) * keys, to], sem.at[s, i, d])

    for d in range(chips):
        for copy in copies(d):
            copy.start()

    token = lax.broadcasted_iota(jnp.int32, (tokens, 8 * chips), 0)
    slot = lax.broadcasted_iota(jnp.int32, (tokens, 8 * chips), 1)
    source, j = jnp.bitwise_xor(here, slot // 8), slot % 4
    place = (2 * source + jnp.bitwise_xor(core, slot % 8 // 4)) * rows + j
    pick = ((place == token) & (j < rows)).astype(jnp.bfloat16)
    gathered = jnp.concatenate([ref[...] for ref in q_refs], axis=0)
    total = jnp.dot(pick, gathered, preferred_element_type=jnp.float32).astype(jnp.bfloat16)
    q_ref[...] = total[:, : chips * width]
    meta_ref[...] = total[:, chips * width :]

    lane = lax.broadcasted_iota(jnp.int32, (tokens, LANES), 1)
    stat_ref[...] = jnp.zeros_like(stat_ref)
    stat = jnp.zeros((tokens, LANES), jnp.float32)
    group = 8
    heads = [(d, h) for d in range(chips) for h in range(heads_dev)]
    for first in range(0, len(heads), group):
        some = heads[first : first + group]
        for d in sorted({d for d, _ in some}):
            for copy in copies(d):
                copy.wait()
        scores = []
        for d, h in some:
            columns = slice(d * width + h * HD, d * width + (h + 1) * HD)
            query = q_ref[:, pl.ds(pl.multiple_of(block(d) * width + h * HD, LANES), HD)]
            scores.append(
                lax.dot_general(query, k_ref[:, columns], (((1,), (1,)), ((), ())), preferred_element_type=jnp.float32)
            )
        expo = []
        for (d, h), score in zip(some, scores):
            peak = jnp.max(score, axis=1, keepdims=True).astype(jnp.bfloat16).astype(jnp.float32)
            weights = jnp.exp2((score - peak) * TO_EXP2)
            rowsum = jnp.sum(weights, axis=1, keepdims=True)
            expo.append(weights.astype(jnp.bfloat16))
            at = d * 2 * heads_dev + h
            stat = jnp.where(lane == at, peak, jnp.where(lane == at + heads_dev, rowsum, stat))
        for i in range(0, len(some), 2):
            columns = slice((first + i) * HD, (first + i + 2) * HD)
            product = jnp.dot(jnp.concatenate(expo[i : i + 2], axis=0), v_ref[:, columns], preferred_element_type=jnp.float32)
            for k in range(2):
                d, h = some[i + k]
                out_ref[block(d), h * tokens : (h + 1) * tokens, :] = product[
                    k * tokens : (k + 1) * tokens, k * HD : (k + 1) * HD
                ].astype(jnp.bfloat16)
    stat_ref[:tokens, :] = stat
    span = 2 * heads_dev
    for tile in range(tiles_of(tokens)):
        turned = stat_ref[tile * LANES : (tile + 1) * LANES, :].T.astype(jnp.bfloat16)
        for d in range(chips):
            out_ref[block(d), main + tile * span : main + (tile + 1) * span, :] = turned[d * span : (d + 1) * span, :]


def project_kernel(tokens, rows, heads_dev, x_ref, w_hbm, meta_ref, mine_ref, other_ref, w_ref, sem):
    me = lax.axis_index("seq")
    core = lax.rem(me, 2)
    chips = x_ref.shape[0]
    step = 512
    chunks = w_hbm.shape[1] // step

    def copy(i):
        at = pl.ds(i * step, step)
        return pltpu.make_async_copy(w_hbm.at[:, at], w_ref.at[:, at], sem.at[i])

    for i in range(chunks):
        copy(i).start()

    main, span = heads_dev * tokens, 2 * heads_dev
    shares = []
    for tile in range(tiles_of(tokens)):
        at = main + tile * span
        stat = [x_ref[i, at : at + span, :].astype(jnp.float32) for i in range(chips)]
        stat = jnp.concatenate(stat + [jnp.zeros((LANES - chips * span, LANES), jnp.float32)], axis=0).T
        stat = jnp.where(lax.broadcasted_iota(jnp.int32, stat.shape, 1) < chips * span, stat, -1e30)
        best, shift = stat, span
        while shift < LANES:
            best = jnp.maximum(best, pltpu.roll(best, shift, 1))
            shift *= 2
        factor = jnp.exp2((stat - best) * TO_EXP2)
        denom, shift = factor * pltpu.roll(stat, LANES - heads_dev, 1), span
        while shift < LANES:
            denom = denom + pltpu.roll(denom, shift, 1)
            shift *= 2
        shares.append(factor / denom)
    share = jnp.concatenate(shares, axis=0)[:tokens, :]
    attended = []
    for h in range(heads_dev):
        total = jnp.zeros((tokens, HD), jnp.float32)
        for i in range(chips):
            at = i * span + h
            total = total + share[:, at : at + 1] * x_ref[i, h * tokens : (h + 1) * tokens, :].astype(jnp.float32)
        attended.append(total.astype(jnp.bfloat16))
    attended = jnp.concatenate(attended, axis=1)

    section = me * heads_dev // HEADS
    control = jnp.minimum(section, CONTROLS - 1)
    is_base = section >= CONTROLS
    meta = meta_ref[...].astype(jnp.float32)
    lane = lax.broadcasted_iota(jnp.int32, meta.shape, 1)

    def column(index):
        return jnp.sum(jnp.where(lane == index, meta, 0.0), axis=1, keepdims=True)

    token = lax.broadcasted_iota(jnp.int32, (tokens, 1), 0)
    owner = column(CONTROLS + control) + BASE * column(2 * CONTROLS + control)
    owner = jnp.where(is_base, token, owner.astype(jnp.int32))
    level = jnp.where(is_base, float(LEVELS), column(control))
    out = lax.broadcasted_iota(jnp.int32, (tokens, 2 * chips * 8), 1)
    j = out % 8
    chip = (out // 8) % chips
    parity = jnp.bitwise_xor(core, out // (8 * chips))
    base = jnp.where(j < rows, (2 * chip + parity) * rows + j, -1)
    selector = (owner == base).astype(jnp.bfloat16)
    turn = (((0,), (0,)), ((), ()))
    mixed = lax.dot_general(selector, attended, turn, preferred_element_type=jnp.float32).astype(jnp.bfloat16)
    wide = jnp.broadcast_to(level, (tokens, LANES)).astype(jnp.bfloat16)
    weight = lax.dot_general(selector, wide, turn, preferred_element_type=jnp.float32)[:, :1] / LEVELS
    for i in range(chunks):
        copy(i).wait()
        at = slice(i * step, (i + 1) * step)
        product = jnp.dot(mixed, w_ref[:, at], preferred_element_type=jnp.float32) * weight
        for c in range(chips):
            mine_ref[c, :, at] = product[8 * c : 8 * c + rows, :].astype(jnp.bfloat16)
            other_ref[c, :, at] = product[8 * (chips + c) : 8 * (chips + c) + rows, :].astype(jnp.bfloat16)


def call(kernel, splits, out_shape, in_specs, scratch, name, limit, args):
    def body(*refs):
        grouped, at = [], 0
        for size in splits:
            grouped.append(refs[at] if size == 0 else refs[at : at + size])
            at += max(size, 1)
        kernel(*grouped, *refs[at:])

    return pl.pallas_call(
        body,
        out_shape=out_shape,
        in_specs=in_specs,
        out_specs=jax.tree.map(lambda _: VMEM, out_shape),
        scratch_shapes=scratch,
        compiler_params=pltpu.CompilerParams(vmem_limit_bytes=limit * 2**20),
        name=name,
    )(*args)


def on_device(queries, key_rows, value_rows, out_weight, levels, owner_map):
    count = lax.axis_size("seq")
    chips, rows = count // 2, queries.shape[0]
    tokens = rows * count
    heads_dev = out_weight.shape[0] // HD
    width = heads_dev * HD
    keys = key_rows.shape[0]
    extra = -(-2 * heads_dev * tiles_of(tokens) // 8) * 8

    def swap(x, bits):
        return lax.ppermute(x, "seq", [(i, i ^ bits) for i in range(count)])

    here = (queries, levels, owner_map)
    there = tuple(swap(x, 1) for x in here)
    key_rows, value_rows, there = lax.optimization_barrier((key_rows, value_rows, there))
    key_there, value_there = swap(key_rows, 1), swap(value_rows, 1)
    packed = call(
        functools.partial(pack_kernel, width),
        (3, 3),
        jax.ShapeDtypeStruct((8, chips * width + LANES), jnp.bfloat16),
        [VMEM, SMEM, SMEM] * 2,
        [],
        "pack",
        56,
        (*here, *there),
    )
    gathered = [packed] + [swap(packed, 2 * d) for d in range(1, chips)]
    groups = [list(range(c, count, 2)) for c in range(2)]

    def exchange(x):
        return lax.all_to_all(x, "seq", split_axis=0, concat_axis=0, axis_index_groups=groups, tiled=True)

    parts, meta = call(
        functools.partial(attend_kernel, tokens, rows, heads_dev),
        (chips, 2, 2),
        [
            jax.ShapeDtypeStruct((chips, heads_dev * tokens + extra, HD), jnp.bfloat16),
            jax.ShapeDtypeStruct((tokens, LANES), jnp.bfloat16),
        ],
        [VMEM] * chips + [IN_HBM] * 4,
        [
            pltpu.VMEM((tokens, chips * width), jnp.bfloat16),
            pltpu.VMEM((2 * keys, chips * width), jnp.bfloat16),
            pltpu.VMEM((2 * keys, chips * width), jnp.bfloat16),
            pltpu.SemaphoreType.DMA((2, 2, chips)),
            pltpu.VMEM((tiles_of(tokens) * LANES, LANES), jnp.float32),
        ],
        "attend",
        61,
        (*gathered, key_rows, key_there, value_rows, value_there),
    )
    share = jax.ShapeDtypeStruct((chips, rows, out_weight.shape[1]), jnp.bfloat16)
    mine, other = call(
        functools.partial(project_kernel, tokens, rows, heads_dev),
        (),
        [share, share],
        [VMEM, IN_HBM, VMEM],
        [pltpu.VMEM(out_weight.shape, out_weight.dtype), pltpu.SemaphoreType.DMA((out_weight.shape[1] // 512,))],
        "project",
        16,
        (exchange(parts), out_weight, meta),
    )
    summed = exchange((mine.astype(jnp.float32) + swap(other, 1).astype(jnp.float32)).astype(jnp.bfloat16))
    return jnp.sum(summed.astype(jnp.float32), axis=0).astype(jnp.bfloat16)


def solution(mesh):
    return jax.shard_map(
        on_device,
        mesh=mesh,
        in_specs=(
            P(("groups", "seq"), None),
            P(("groups", "seq"), None),
            P(("groups", "seq"), None),
            P("seq", None),
            P(None, ("groups", "seq")),
            P(None, ("groups", "seq")),
        ),
        out_specs=P(("groups", "seq"), None),
        check_vma=False,
    )
```

```python
import functools

import jax
import jax.numpy as jnp
from jax import lax
from jax.experimental import pallas as pl
from jax.experimental.pallas import tpu as pltpu
from jax.sharding import PartitionSpec as P

HD = 128
HEADS = 16
CONTROLS = 3
LEVELS = 8
LANES = 128
BASE = 256
GROUPS = 4
TO_EXP2 = HD ** (-0.5) * 1.4426950408889634

PACK_MIB, ATTEND_MIB, PROJECT_MIB = 56, 61, 61

VMEM = pl.BlockSpec(memory_space=pltpu.VMEM)
SMEM = pl.BlockSpec(memory_space=pltpu.SMEM)
IN_HBM = pl.BlockSpec(memory_space=pltpu.HBM)


def tiles_of(tokens):
    return -(-tokens // LANES)


def pack_kernel(width, here_refs, there_refs, out_ref):
    core = lax.rem(lax.axis_index("seq"), 2)
    chips, height = out_ref.shape[:2]
    rows, lanes = here_refs[0].shape[0], out_ref.shape[2] - LANES
    row = lax.broadcasted_iota(jnp.int32, (height, lanes), 0)
    meta_row = lax.broadcasted_iota(jnp.int32, (height, LANES), 0)
    meta_lane = lax.broadcasted_iota(jnp.int32, (height, LANES), 1)
    packed = jnp.zeros((height, lanes), jnp.float32)
    meta = jnp.zeros((height, LANES), jnp.int32)
    for i, (q_ref, level_ref, owner_ref) in enumerate((here_refs, there_refs)):
        mine = [
            q_ref[:, pl.ds(pl.multiple_of((2 * chip + core) * width, LANES), width)].astype(jnp.float32)
            for chip in range(chips)
        ]
        mine = jnp.concatenate(mine, axis=1)
        for t in range(rows):
            token = i * rows + t
            for c in range(CONTROLS):
                owner = owner_ref[c, t]
                for index, value in (
                    (c, level_ref[c, t]), (CONTROLS + c, owner & (BASE - 1)), (2 * CONTROLS + c, owner >> 8)
                ):
                    meta = jnp.where((meta_row == token) & (meta_lane == index), value, meta)
            for g in range(GROUPS):
                packed = jnp.where(
                    row == g * 2 * rows + token, mine[t : t + 1, g * lanes : (g + 1) * lanes], packed
                )
    packed = packed.astype(jnp.bfloat16)
    meta = meta.astype(jnp.float32).astype(jnp.bfloat16)
    for chip in range(chips):
        out_ref[chip, :, :lanes] = packed
        out_ref[chip, :, lanes:] = meta


def attend_kernel(tokens, rows, heads_dev, in_ref, key_refs, value_refs, out_ref, meta_ref, q_ref, k_ref, v_ref, sem, stat_ref):
    me = lax.axis_index("seq")
    core, here = lax.rem(me, 2), me // 2
    chips = out_ref.shape[0]
    width = heads_dev * HD
    keys = key_refs[0].shape[0]
    main = heads_dev * tokens

    def block(d):
        return jnp.bitwise_xor(here, d)

    def copies(d):
        at = pl.ds(pl.multiple_of((2 * block(d) + core) * width, LANES), width)
        to = pl.ds(d * width, width)
        for s, refs, buffer in ((0, key_refs, k_ref), (1, value_refs, v_ref)):
            for i, ref in enumerate(refs):
                yield pltpu.make_async_copy(ref.at[:, at], buffer.at[i * keys : (i + 1) * keys, to], sem.at[s, i, d])

    for d in range(chips):
        for copy in copies(d):
            copy.start()

    height, lanes = in_ref.shape[0] // chips, in_ref.shape[1] - LANES
    token = lax.broadcasted_iota(jnp.int32, (tokens, in_ref.shape[0]), 0)
    slot = lax.broadcasted_iota(jnp.int32, (tokens, in_ref.shape[0]), 1)
    source, at = slot // height, slot % height
    owner_core = jnp.bitwise_xor(core, at // rows % 2)
    same = (2 * source + owner_core) * rows + at % rows == token
    for g in range(GROUPS):
        pick = (same & (at // (2 * rows) == g)).astype(jnp.bfloat16)
        q_ref[:, g * lanes : (g + 1) * lanes] = jnp.dot(
            pick, in_ref[:, :lanes], preferred_element_type=jnp.float32
        ).astype(jnp.bfloat16)
        if g == 0:
            meta_ref[...] = jnp.dot(pick, in_ref[:, lanes:], preferred_element_type=jnp.float32).astype(jnp.bfloat16)

    lane = lax.broadcasted_iota(jnp.int32, (tokens, LANES), 1)
    stat_ref[...] = jnp.zeros_like(stat_ref)
    stat = jnp.zeros((tokens, LANES), jnp.float32)
    group = 8
    heads = [(d, h) for d in range(chips) for h in range(heads_dev)]
    for first in range(0, len(heads), group):
        some = heads[first : first + group]
        for d in sorted({d for d, _ in some}):
            for copy in copies(d):
                copy.wait()
        scores = []
        for d, h in some:
            columns = slice(d * width + h * HD, d * width + (h + 1) * HD)
            query = q_ref[:, pl.ds(pl.multiple_of(block(d) * width + h * HD, LANES), HD)]
            scores.append(
                lax.dot_general(query, k_ref[:, columns], (((1,), (1,)), ((), ())), preferred_element_type=jnp.float32)
            )
        expo = []
        for (d, h), score in zip(some, scores):
            peak = jnp.max(score, axis=1, keepdims=True).astype(jnp.bfloat16).astype(jnp.float32)
            weights = jnp.exp2((score - peak) * TO_EXP2)
            rowsum = jnp.sum(weights, axis=1, keepdims=True)
            expo.append(weights.astype(jnp.bfloat16))
            at = d * 2 * heads_dev + h
            stat = jnp.where(lane == at, peak, jnp.where(lane == at + heads_dev, rowsum, stat))
        for i in range(0, len(some), 2):
            columns = slice((first + i) * HD, (first + i + 2) * HD)
            product = jnp.dot(jnp.concatenate(expo[i : i + 2], axis=0), v_ref[:, columns], preferred_element_type=jnp.float32)
            for k in range(2):
                d, h = some[i + k]
                out_ref[block(d), h * tokens : (h + 1) * tokens, :] = product[
                    k * tokens : (k + 1) * tokens, k * HD : (k + 1) * HD
                ].astype(jnp.bfloat16)
    stat_ref[:tokens, :] = stat
    span = 2 * heads_dev
    for tile in range(tiles_of(tokens)):
        turned = stat_ref[tile * LANES : (tile + 1) * LANES, :].T.astype(jnp.bfloat16)
        for d in range(chips):
            out_ref[block(d), main + tile * span : main + (tile + 1) * span, :] = turned[d * span : (d + 1) * span, :]


def project_kernel(tokens, rows, heads_dev, x_ref, w_hbm, meta_ref, mine_ref, other_ref, w_ref, sem):
    me = lax.axis_index("seq")
    core = lax.rem(me, 2)
    chips = x_ref.shape[0]
    step = 512
    chunks = w_hbm.shape[1] // step

    def copy(i):
        at = pl.ds(i * step, step)
        return pltpu.make_async_copy(w_hbm.at[:, at], w_ref.at[:, at], sem.at[i])

    for i in range(chunks):
        copy(i).start()

    main, span = heads_dev * tokens, 2 * heads_dev
    shares = []
    for tile in range(tiles_of(tokens)):
        at = main + tile * span
        stat = [x_ref[i, at : at + span, :].astype(jnp.float32) for i in range(chips)]
        stat = jnp.concatenate(stat + [jnp.zeros((LANES - chips * span, LANES), jnp.float32)], axis=0).T
        stat = jnp.where(lax.broadcasted_iota(jnp.int32, stat.shape, 1) < chips * span, stat, -1e30)
        best, shift = stat, span
        while shift < LANES:
            best = jnp.maximum(best, pltpu.roll(best, shift, 1))
            shift *= 2
        factor = jnp.exp2((stat - best) * TO_EXP2)
        denom, shift = factor * pltpu.roll(stat, LANES - heads_dev, 1), span
        while shift < LANES:
            denom = denom + pltpu.roll(denom, shift, 1)
            shift *= 2
        shares.append(factor / denom)
    share = jnp.concatenate(shares, axis=0)[:tokens, :]
    attended = []
    for h in range(heads_dev):
        total = jnp.zeros((tokens, HD), jnp.float32)
        for i in range(chips):
            at = i * span + h
            total = total + share[:, at : at + 1] * x_ref[i, h * tokens : (h + 1) * tokens, :].astype(jnp.float32)
        attended.append(total.astype(jnp.bfloat16))
    attended = jnp.concatenate(attended, axis=1)

    section = me * heads_dev // HEADS
    control = jnp.minimum(section, CONTROLS - 1)
    is_base = section >= CONTROLS
    meta = meta_ref[...].astype(jnp.float32)
    lane = lax.broadcasted_iota(jnp.int32, meta.shape, 1)

    def column(index):
        return jnp.sum(jnp.where(lane == index, meta, 0.0), axis=1, keepdims=True)

    token = lax.broadcasted_iota(jnp.int32, (tokens, 1), 0)
    owner = column(CONTROLS + control) + BASE * column(2 * CONTROLS + control)
    owner = jnp.where(is_base, token, owner.astype(jnp.int32))
    level = jnp.where(is_base, float(LEVELS), column(control))
    out = lax.broadcasted_iota(jnp.int32, (tokens, 2 * chips * 8), 1)
    j = out % 8
    chip = (out // 8) % chips
    parity = jnp.bitwise_xor(core, out // (8 * chips))
    base = jnp.where(j < rows, (2 * chip + parity) * rows + j, -1)
    selector = (owner == base).astype(jnp.bfloat16)
    turn = (((0,), (0,)), ((), ()))
    mixed = lax.dot_general(selector, attended, turn, preferred_element_type=jnp.float32).astype(jnp.bfloat16)
    wide = jnp.broadcast_to(level, (tokens, LANES)).astype(jnp.bfloat16)
    weight = lax.dot_general(selector, wide, turn, preferred_element_type=jnp.float32)[:, :1] / LEVELS
    for i in range(chunks):
        copy(i).wait()
        at = slice(i * step, (i + 1) * step)
        product = jnp.dot(mixed, w_ref[:, at], preferred_element_type=jnp.float32) * weight
        for c in range(chips):
            mine_ref[c, :, at] = product[8 * c : 8 * c + rows, :].astype(jnp.bfloat16)
            other_ref[c, :, at] = product[8 * (chips + c) : 8 * (chips + c) + rows, :].astype(jnp.bfloat16)


def call(kernel, splits, out_shape, in_specs, scratch, name, limit, args):
    def body(*refs):
        grouped, at = [], 0
        for size in splits:
            grouped.append(refs[at] if size == 0 else refs[at : at + size])
            at += max(size, 1)
        kernel(*grouped, *refs[at:])

    return pl.pallas_call(
        body,
        out_shape=out_shape,
        in_specs=in_specs,
        out_specs=jax.tree.map(lambda _: VMEM, out_shape),
        scratch_shapes=scratch,
        compiler_params=pltpu.CompilerParams(vmem_limit_bytes=limit * 2**20),
        name=name,
    )(*args)


def on_device(queries, key_rows, value_rows, out_weight, levels, owner_map):
    count = lax.axis_size("seq")
    chips, rows = count // 2, queries.shape[0]
    tokens = rows * count
    heads_dev = out_weight.shape[0] // HD
    width = heads_dev * HD
    keys = key_rows.shape[0]
    extra = -(-2 * heads_dev * tiles_of(tokens) // 8) * 8

    def swap(x, bits):
        return lax.ppermute(x, "seq", [(i, i ^ bits) for i in range(count)])

    here = (queries, levels, owner_map)
    there = tuple(swap(x, 1) for x in here)
    key_rows, value_rows, there = lax.optimization_barrier((key_rows, value_rows, there))
    key_there, value_there = swap(key_rows, 1), swap(value_rows, 1)
    groups = [list(range(c, count, 2)) for c in range(2)]

    def exchange(x):
        return lax.all_to_all(x, "seq", split_axis=0, concat_axis=0, axis_index_groups=groups, tiled=True)

    height, lanes = GROUPS * 2 * rows, chips * width // GROUPS + LANES
    packed = call(
        functools.partial(pack_kernel, width),
        (3, 3),
        jax.ShapeDtypeStruct((chips, height, lanes), jnp.bfloat16),
        [VMEM, SMEM, SMEM] * 2,
        [],
        "pack",
        PACK_MIB,
        (*here, *there),
    )
    gathered = exchange(packed).reshape(chips * height, lanes)
    parts, meta = call(
        functools.partial(attend_kernel, tokens, rows, heads_dev),
        (0, 2, 2),
        [
            jax.ShapeDtypeStruct((chips, heads_dev * tokens + extra, HD), jnp.bfloat16),
            jax.ShapeDtypeStruct((tokens, LANES), jnp.bfloat16),
        ],
        [VMEM] + [IN_HBM] * 4,
        [
            pltpu.VMEM((tokens, chips * width), jnp.bfloat16),
            pltpu.VMEM((2 * keys, chips * width), jnp.bfloat16),
            pltpu.VMEM((2 * keys, chips * width), jnp.bfloat16),
            pltpu.SemaphoreType.DMA((2, 2, chips)),
            pltpu.VMEM((tiles_of(tokens) * LANES, LANES), jnp.float32),
        ],
        "attend",
        ATTEND_MIB,
        (gathered, key_rows, key_there, value_rows, value_there),
    )
    share = jax.ShapeDtypeStruct((chips, rows, out_weight.shape[1]), jnp.bfloat16)
    mine, other = call(
        functools.partial(project_kernel, tokens, rows, heads_dev),
        (),
        [share, share],
        [VMEM, IN_HBM, VMEM],
        [pltpu.VMEM(out_weight.shape, out_weight.dtype), pltpu.SemaphoreType.DMA((out_weight.shape[1] // 512,))],
        "project",
        PROJECT_MIB,
        (exchange(parts), out_weight, meta),
    )
    summed = exchange((mine.astype(jnp.float32) + swap(other, 1).astype(jnp.float32)).astype(jnp.bfloat16))
    return jnp.sum(summed.astype(jnp.float32), axis=0).astype(jnp.bfloat16)


def solution(mesh):
    return jax.shard_map(
        on_device,
        mesh=mesh,
        in_specs=(
            P(("groups", "seq"), None),
            P(("groups", "seq"), None),
            P(("groups", "seq"), None),
            P("seq", None),
            P(None, ("groups", "seq")),
            P(None, ("groups", "seq")),
        ),
        out_specs=P(("groups", "seq"), None),
        check_vma=False,
    )
```

```python
import functools

import jax
import jax.numpy as jnp
from jax import lax
from jax.experimental import pallas as pl
from jax.experimental.pallas import tpu as pltpu
from jax.sharding import PartitionSpec as P

HD = 128
HEADS = 16
CONTROLS = 3
LEVELS = 8
LANES = 128
BASE = 256
GROUPS = 4
TO_EXP2 = HD ** (-0.5) * 1.4426950408889634

PACK_MIB, ATTEND_MIB, PROJECT_MIB = 61, 24, 16


VMEM = pl.BlockSpec(memory_space=pltpu.VMEM)
SMEM = pl.BlockSpec(memory_space=pltpu.SMEM)
IN_HBM = pl.BlockSpec(memory_space=pltpu.HBM)


def tiles_of(tokens, rows):
    return -(-(tokens + 2 * rows * 3 * CONTROLS) // LANES)


def pack_kernel(width, here_ref, there_ref, out_ref):
    core = lax.rem(lax.axis_index("seq"), 2)
    height, lanes = out_ref.shape
    rows, chips = here_ref.shape[0], here_ref.shape[1] // (2 * width)
    row = lax.broadcasted_iota(jnp.int32, (height, lanes), 0)
    packed = jnp.zeros((height, lanes), jnp.float32)
    for i, q_ref in enumerate((here_ref, there_ref)):
        mine = [
            q_ref[:, pl.ds(pl.multiple_of((2 * chip + core) * width, LANES), width)].astype(jnp.float32)
            for chip in range(chips)
        ]
        mine = jnp.concatenate(mine, axis=1)
        for t in range(rows):
            for g in range(GROUPS):
                packed = jnp.where(
                    row == g * 2 * rows + i * rows + t, mine[t : t + 1, g * lanes : (g + 1) * lanes], packed
                )
    out_ref[...] = packed.astype(jnp.bfloat16)


def attend_kernel(tokens, rows, heads_dev, in_refs, key_refs, value_refs, level_refs, owner_refs, out_ref, q_ref, k_ref, v_ref, sem, stat_ref):
    me = lax.axis_index("seq")
    core, here = lax.rem(me, 2), me // 2
    chips = out_ref.shape[0]
    width = heads_dev * HD
    keys = key_refs[0].shape[0]
    main = heads_dev * tokens

    def block(d):
        return jnp.bitwise_xor(here, d)

    def copies(d):
        at = pl.ds(pl.multiple_of((2 * block(d) + core) * width, LANES), width)
        to = pl.ds(d * width, width)
        for s, refs, buffer in ((0, key_refs, k_ref), (1, value_refs, v_ref)):
            for i, ref in enumerate(refs):
                yield pltpu.make_async_copy(ref.at[:, at], buffer.at[i * keys : (i + 1) * keys, to], sem.at[s, i, d])

    for d in range(chips):
        for copy in copies(d):
            copy.start()

    height, lanes = in_refs[0].shape
    token = lax.broadcasted_iota(jnp.int32, (tokens, chips * height), 0)
    slot = lax.broadcasted_iota(jnp.int32, (tokens, chips * height), 1)
    source, at = block(slot // height), slot % height
    owner_core = jnp.bitwise_xor(core, at // rows % 2)
    same = (2 * source + owner_core) * rows + at % rows == token
    gathered = jnp.concatenate([ref[...] for ref in in_refs], axis=0)
    for g in range(GROUPS):
        pick = (same & (at // (2 * rows) == g)).astype(jnp.bfloat16)
        q_ref[:, g * lanes : (g + 1) * lanes] = jnp.dot(pick, gathered, preferred_element_type=jnp.float32).astype(
            jnp.bfloat16
        )

    lane = lax.broadcasted_iota(jnp.int32, (tokens, LANES), 1)
    stat_ref[...] = jnp.zeros_like(stat_ref)
    stat = jnp.zeros((tokens, LANES), jnp.float32)
    group = 8
    heads = [(d, h) for d in range(chips) for h in range(heads_dev)]
    for first in range(0, len(heads), group):
        some = heads[first : first + group]
        for d in sorted({d for d, _ in some}):
            for copy in copies(d):
                copy.wait()
        scores = []
        for d, h in some:
            columns = slice(d * width + h * HD, d * width + (h + 1) * HD)
            query = q_ref[:, pl.ds(pl.multiple_of(block(d) * width + h * HD, LANES), HD)]
            scores.append(
                lax.dot_general(query, k_ref[:, columns], (((1,), (1,)), ((), ())), preferred_element_type=jnp.float32)
            )
        expo = []
        for (d, h), score in zip(some, scores):
            peak = jnp.max(score, axis=1, keepdims=True).astype(jnp.bfloat16).astype(jnp.float32)
            weights = jnp.exp2((score - peak) * TO_EXP2)
            rowsum = jnp.sum(weights, axis=1, keepdims=True)
            expo.append(weights.astype(jnp.bfloat16))
            at = d * 2 * heads_dev + h
            stat = jnp.where(lane == at, peak, jnp.where(lane == at + heads_dev, rowsum, stat))
        for i in range(0, len(some), 2):
            columns = slice((first + i) * HD, (first + i + 2) * HD)
            product = jnp.dot(jnp.concatenate(expo[i : i + 2], axis=0), v_ref[:, columns], preferred_element_type=jnp.float32)
            for k in range(2):
                d, h = some[i + k]
                out_ref[block(d), h * tokens : (h + 1) * tokens, :] = product[
                    k * tokens : (k + 1) * tokens, k * HD : (k + 1) * HD
                ].astype(jnp.bfloat16)
    stat_ref[:tokens, :] = stat
    at = tokens
    for level_ref, owner_ref in zip(level_refs, owner_refs):
        for t in range(rows):
            for c in range(CONTROLS):
                owner = owner_ref[c, t]
                for value in (level_ref[c, t], owner & (BASE - 1), owner >> 8):
                    stat_ref[at : at + 1, :] = jnp.full((1, LANES), value, jnp.int32).astype(jnp.float32)
                    at += 1
    span = 2 * heads_dev
    for tile in range(tiles_of(tokens, rows)):
        turned = stat_ref[tile * LANES : (tile + 1) * LANES, :].T.astype(jnp.bfloat16)
        for d in range(chips):
            out_ref[block(d), main + tile * span : main + (tile + 1) * span, :] = turned[d * span : (d + 1) * span, :]


def project_kernel(tokens, rows, heads_dev, x_ref, w_ref, mine_ref, other_ref):
    me = lax.axis_index("seq")
    core = lax.rem(me, 2)
    chips = x_ref.shape[0]
    main, span = heads_dev * tokens, 2 * heads_dev
    stats, shares = [], []
    for tile in range(tiles_of(tokens, rows)):
        at = main + tile * span
        stat = [x_ref[i, at : at + span, :].astype(jnp.float32) for i in range(chips)]
        stat = jnp.concatenate(stat + [jnp.zeros((LANES - chips * span, LANES), jnp.float32)], axis=0).T
        stats.append(stat)
        stat = jnp.where(lax.broadcasted_iota(jnp.int32, stat.shape, 1) < chips * span, stat, -1e30)
        best, shift = stat, span
        while shift < LANES:
            best = jnp.maximum(best, pltpu.roll(best, shift, 1))
            shift *= 2
        factor = jnp.exp2((stat - best) * TO_EXP2)
        denom, shift = factor * pltpu.roll(stat, LANES - heads_dev, 1), span
        while shift < LANES:
            denom = denom + pltpu.roll(denom, shift, 1)
            shift *= 2
        shares.append(factor / denom)
    share = jnp.concatenate(shares, axis=0)[:tokens, :]
    attended = []
    for h in range(heads_dev):
        total = jnp.zeros((tokens, HD), jnp.float32)
        for i in range(chips):
            at = i * span + h
            total = total + share[:, at : at + 1] * x_ref[i, h * tokens : (h + 1) * tokens, :].astype(jnp.float32)
        attended.append(total.astype(jnp.bfloat16))
    attended = jnp.concatenate(attended, axis=1)

    section = me * heads_dev // HEADS
    control = jnp.minimum(section, CONTROLS - 1)
    is_base = section >= CONTROLS
    meta = jnp.concatenate(stats, axis=0)
    token = lax.broadcasted_iota(jnp.int32, (tokens, LANES), 0)
    lane = lax.broadcasted_iota(jnp.int32, (tokens, LANES), 1)
    level = jnp.zeros((tokens, LANES), jnp.float32)
    owner = jnp.zeros((tokens, LANES), jnp.float32)
    for s in range(2 * rows):
        place = (2 * (lane // span) + jnp.bitwise_xor(core, s // rows)) * rows + s % rows
        here = (place == token) & (lane % span == 0)
        for c in range(CONTROLS):
            at = tokens + (s * CONTROLS + c) * 3
            mask = here & (control == c)
            level = jnp.where(mask, meta[at : at + 1, :], level)
            owner = jnp.where(mask, meta[at + 1 : at + 2, :] + BASE * meta[at + 2 : at + 3, :], owner)
    level = jnp.sum(level, axis=1, keepdims=True)
    owner = jnp.sum(owner, axis=1, keepdims=True).astype(jnp.int32)
    owner = jnp.where(is_base, token[:, :1], owner)
    level = jnp.where(is_base, float(LEVELS), level)
    out = lax.broadcasted_iota(jnp.int32, (tokens, 2 * chips * 8), 1)
    j = out % 8
    chip = (out // 8) % chips
    parity = jnp.bitwise_xor(core, out // (8 * chips))
    base = jnp.where(j < rows, (2 * chip + parity) * rows + j, -1)
    selector = (owner == base).astype(jnp.bfloat16)
    turn = (((0,), (0,)), ((), ()))
    mixed = lax.dot_general(selector, attended, turn, preferred_element_type=jnp.float32).astype(jnp.bfloat16)
    wide = jnp.broadcast_to(level, (tokens, LANES)).astype(jnp.bfloat16)
    weight = lax.dot_general(selector, wide, turn, preferred_element_type=jnp.float32)[:, :1] / LEVELS
    step = 512
    for i in range(w_ref.shape[1] // step):
        at = slice(i * step, (i + 1) * step)
        product = jnp.dot(mixed, w_ref[:, at], preferred_element_type=jnp.float32) * weight
        for c in range(chips):
            mine_ref[c, :, at] = product[8 * c : 8 * c + rows, :].astype(jnp.bfloat16)
            other_ref[c, :, at] = product[8 * (chips + c) : 8 * (chips + c) + rows, :].astype(jnp.bfloat16)


def call(kernel, splits, out_shape, in_specs, scratch, name, limit, args):
    def body(*refs):
        grouped, at = [], 0
        for size in splits:
            grouped.append(refs[at] if size == 0 else refs[at : at + size])
            at += max(size, 1)
        kernel(*grouped, *refs[at:])

    return pl.pallas_call(
        body,
        out_shape=out_shape,
        in_specs=in_specs,
        out_specs=jax.tree.map(lambda _: VMEM, out_shape),
        scratch_shapes=scratch,
        compiler_params=pltpu.CompilerParams(vmem_limit_bytes=limit * 2**20),
        name=name,
    )(*args)


def on_device(queries, key_rows, value_rows, out_weight, levels, owner_map):
    count = lax.axis_size("seq")
    chips, rows = count // 2, queries.shape[0]
    tokens = rows * count
    heads_dev = out_weight.shape[0] // HD
    width = heads_dev * HD
    keys = key_rows.shape[0]
    extra = -(-2 * heads_dev * tiles_of(tokens, rows) // 8) * 8

    def swap(x, bits):
        return lax.ppermute(x, "seq", [(i, i ^ bits) for i in range(count)])

    there = swap(queries, 1)
    level_there, owner_there = swap(levels, 1), swap(owner_map, 1)
    key_rows, value_rows, there, level_there, owner_there = lax.optimization_barrier(
        (key_rows, value_rows, there, level_there, owner_there)
    )
    rest = [key_rows, swap(key_rows, 1), value_rows, swap(value_rows, 1), levels, level_there, owner_map, owner_there]
    rest = [pltpu.with_memory_space_constraint(x, pltpu.HBM) for x in rest]
    groups = [list(range(c, count, 2)) for c in range(2)]

    def exchange(x):
        return lax.all_to_all(x, "seq", split_axis=0, concat_axis=0, axis_index_groups=groups, tiled=True)

    packed = call(
        functools.partial(pack_kernel, width),
        (),
        jax.ShapeDtypeStruct((GROUPS * 2 * rows, chips * width // GROUPS), jnp.bfloat16),
        [VMEM] * 2,
        [],
        "pack",
        PACK_MIB,
        (queries, there),
    )
    gathered = [pltpu.with_memory_space_constraint(packed, pltpu.HBM)] + [swap(packed, 2 * d) for d in range(1, chips)]
    parts = call(
        functools.partial(attend_kernel, tokens, rows, heads_dev),
        (chips, 2, 2, 2, 2),
        jax.ShapeDtypeStruct((chips, heads_dev * tokens + extra, HD), jnp.bfloat16),
        [VMEM] * chips + [IN_HBM] * 4 + [SMEM] * 4,
        [
            pltpu.VMEM((tokens, chips * width), jnp.bfloat16),
            pltpu.VMEM((2 * keys, chips * width), jnp.bfloat16),
            pltpu.VMEM((2 * keys, chips * width), jnp.bfloat16),
            pltpu.SemaphoreType.DMA((2, 2, chips)),
            pltpu.VMEM((tiles_of(tokens, rows) * LANES, LANES), jnp.float32),
        ],
        "attend",
        ATTEND_MIB,
        (*gathered, *rest),
    )
    share = jax.ShapeDtypeStruct((chips, rows, out_weight.shape[1]), jnp.bfloat16)
    mine, other = call(
        functools.partial(project_kernel, tokens, rows, heads_dev),
        (),
        [share, share],
        [VMEM, VMEM],
        [],
        "project",
        PROJECT_MIB,
        (exchange(parts), out_weight),
    )
    summed = exchange((mine.astype(jnp.float32) + swap(other, 1).astype(jnp.float32)).astype(jnp.bfloat16))
    return jnp.sum(summed.astype(jnp.float32), axis=0).astype(jnp.bfloat16)


def solution(mesh):
    return jax.shard_map(
        on_device,
        mesh=mesh,
        in_specs=(
            P(("groups", "seq"), None),
            P(("groups", "seq"), None),
            P(("groups", "seq"), None),
            P("seq", None),
            P(None, ("groups", "seq")),
            P(None, ("groups", "seq")),
        ),
        out_specs=P(("groups", "seq"), None),
        check_vma=False,
    )
```

```python
import functools

import jax
import jax.numpy as jnp
from jax import lax
from jax.experimental import pallas as pl
from jax.experimental.pallas import tpu as pltpu
from jax.sharding import PartitionSpec as P


HD = 128
HEADS = 16
CONTROLS = 3
LEVELS = 8
LANES = 128
BASE = 256
GROUPS = 4
TO_EXP2 = HD ** (-0.5) * 1.4426950408889634

PACK_MIB, ATTEND_MIB, PROJECT_MIB = 61, 24, 16


VMEM = pl.BlockSpec(memory_space=pltpu.VMEM)
SMEM = pl.BlockSpec(memory_space=pltpu.SMEM)
IN_HBM = pl.BlockSpec(memory_space=pltpu.HBM)


def tiles_of(tokens, rows):
    return -(-(tokens + 2 * rows * 3 * CONTROLS) // LANES)


def pack_kernel(width, here_ref, there_ref, out_ref):
    core = lax.rem(lax.axis_index("seq"), 2)
    height, lanes = out_ref.shape
    rows, chips = here_ref.shape[0], here_ref.shape[1] // (2 * width)
    row = lax.broadcasted_iota(jnp.int32, (height, lanes), 0)
    packed = jnp.zeros((height, lanes), jnp.float32)
    for i, q_ref in enumerate((here_ref, there_ref)):
        mine = [
            q_ref[:, pl.ds(pl.multiple_of((2 * chip + core) * width, LANES), width)].astype(jnp.float32)
            for chip in range(chips)
        ]
        mine = jnp.concatenate(mine, axis=1)
        for t in range(rows):
            for g in range(GROUPS):
                packed = jnp.where(
                    row == g * 2 * rows + i * rows + t, mine[t : t + 1, g * lanes : (g + 1) * lanes], packed
                )
    out_ref[...] = packed.astype(jnp.bfloat16)


def attend_kernel(tokens, rows, heads_dev, in_refs, key_refs, value_refs, level_refs, owner_refs, out_refs, q_ref, k_ref, v_ref, sem, stat_ref):
    me = lax.axis_index("seq")
    core, here = lax.rem(me, 2), me // 2
    chips = len(out_refs)
    width = heads_dev * HD
    keys = key_refs[0].shape[0]
    main = heads_dev * tokens

    def block(d):
        return jnp.bitwise_xor(here, d)

    def copies(d):
        at = pl.ds(pl.multiple_of((2 * block(d) + core) * width, LANES), width)
        to = pl.ds(d * width, width)
        for s, refs, buffer in ((0, key_refs, k_ref), (1, value_refs, v_ref)):
            for i, ref in enumerate(refs):
                yield pltpu.make_async_copy(ref.at[:, at], buffer.at[i * keys : (i + 1) * keys, to], sem.at[s, i, d])

    for d in range(chips):
        for copy in copies(d):
            copy.start()

    _, lanes = in_refs[0].shape
    for g in range(GROUPS):
        low, high = g * 2 * rows // 8 * 8, -(-(g + 1) * 2 * rows // 8) * 8
        some = high - low
        gathered = jnp.concatenate([ref[low:high, :] for ref in in_refs], axis=0)
        token = lax.broadcasted_iota(jnp.int32, (tokens, chips * some), 0)
        slot = lax.broadcasted_iota(jnp.int32, (tokens, chips * some), 1)
        at = low + slot % some - g * 2 * rows
        owner_core = jnp.bitwise_xor(core, jnp.where(at >= rows, 1, 0))
        place = (2 * block(slot // some) + owner_core) * rows + jnp.where(at >= rows, at - rows, at)
        pick = ((place == token) & (at >= 0) & (at < 2 * rows)).astype(jnp.bfloat16)
        q_ref[:, g * lanes : (g + 1) * lanes] = jnp.dot(pick, gathered, preferred_element_type=jnp.float32).astype(
            jnp.bfloat16
        )

    lane = lax.broadcasted_iota(jnp.int32, (tokens, LANES), 1)
    stat_ref[...] = jnp.zeros_like(stat_ref)
    stat = jnp.zeros((tokens, LANES), jnp.float32)
    group = 8
    heads = [(d, h) for d in range(chips) for h in range(heads_dev)]
    for first in range(0, len(heads), group):
        some = heads[first : first + group]
        for d in sorted({d for d, _ in some}):
            for copy in copies(d):
                copy.wait()
        scores = []
        for d, h in some:
            columns = slice(d * width + h * HD, d * width + (h + 1) * HD)
            query = q_ref[:, pl.ds(pl.multiple_of(block(d) * width + h * HD, LANES), HD)]
            scores.append(
                lax.dot_general(query, k_ref[:, columns], (((1,), (1,)), ((), ())), preferred_element_type=jnp.float32)
            )
        expo = []
        for (d, h), score in zip(some, scores):
            peak = jnp.max(score, axis=1, keepdims=True).astype(jnp.bfloat16).astype(jnp.float32)
            weights = jnp.exp2((score - peak) * TO_EXP2)
            rowsum = jnp.sum(weights, axis=1, keepdims=True)
            expo.append(weights.astype(jnp.bfloat16))
            at = d * 2 * heads_dev + h
            stat = jnp.where(lane == at, peak, jnp.where(lane == at + heads_dev, rowsum, stat))
        for i in range(0, len(some), 2):
            columns = slice((first + i) * HD, (first + i + 2) * HD)
            product = jnp.dot(jnp.concatenate(expo[i : i + 2], axis=0), v_ref[:, columns], preferred_element_type=jnp.float32)
            for k in range(2):
                d, h = some[i + k]
                out_refs[d][h * tokens : (h + 1) * tokens, :] = product[
                    k * tokens : (k + 1) * tokens, k * HD : (k + 1) * HD
                ].astype(jnp.bfloat16)
    stat_ref[:tokens, :] = stat
    at = tokens
    for level_ref, owner_ref in zip(level_refs, owner_refs):
        for t in range(rows):
            for c in range(CONTROLS):
                owner = owner_ref[c, t]
                for value in (level_ref[c, t], owner & (BASE - 1), owner >> 8):
                    stat_ref[at : at + 1, :] = jnp.full((1, LANES), value, jnp.int32).astype(jnp.float32)
                    at += 1
    span = 2 * heads_dev
    for tile in range(tiles_of(tokens, rows)):
        turned = stat_ref[tile * LANES : (tile + 1) * LANES, :].T.astype(jnp.bfloat16)
        for d in range(chips):
            out_refs[d][main + tile * span : main + (tile + 1) * span, :] = turned[d * span : (d + 1) * span, :]


def project_kernel(tokens, rows, heads_dev, x_refs, w_ref, mine_ref, other_ref):
    me = lax.axis_index("seq")
    core = lax.rem(me, 2)
    chips = len(x_refs)
    main, span = heads_dev * tokens, 2 * heads_dev
    stats, shares = [], []
    for tile in range(tiles_of(tokens, rows)):
        at = main + tile * span
        stat = [x_refs[i][at : at + span, :].astype(jnp.float32) for i in range(chips)]
        stat = jnp.concatenate(stat + [jnp.zeros((LANES - chips * span, LANES), jnp.float32)], axis=0).T
        stats.append(stat)
        stat = jnp.where(lax.broadcasted_iota(jnp.int32, stat.shape, 1) < chips * span, stat, -1e30)
        best, shift = stat, span
        while shift < LANES:
            best = jnp.maximum(best, pltpu.roll(best, shift, 1))
            shift *= 2
        factor = jnp.exp2((stat - best) * TO_EXP2)
        denom, shift = factor * pltpu.roll(stat, LANES - heads_dev, 1), span
        while shift < LANES:
            denom = denom + pltpu.roll(denom, shift, 1)
            shift *= 2
        shares.append(factor / denom)
    share = jnp.concatenate(shares, axis=0)[:tokens, :]
    attended = []
    for h in range(heads_dev):
        total = jnp.zeros((tokens, HD), jnp.float32)
        for i in range(chips):
            at = i * span + h
            total = total + share[:, at : at + 1] * x_refs[i][h * tokens : (h + 1) * tokens, :].astype(jnp.float32)
        attended.append(total.astype(jnp.bfloat16))
    attended = jnp.concatenate(attended, axis=1)

    section = me * heads_dev // HEADS
    control = jnp.minimum(section, CONTROLS - 1)
    is_base = section >= CONTROLS
    meta = jnp.concatenate(stats, axis=0)
    token = lax.broadcasted_iota(jnp.int32, (tokens, LANES), 0)
    lane = lax.broadcasted_iota(jnp.int32, (tokens, LANES), 1)
    level = jnp.zeros((tokens, LANES), jnp.float32)
    owner = jnp.zeros((tokens, LANES), jnp.float32)
    for s in range(2 * rows):
        place = (2 * jnp.bitwise_xor(me // 2, lane // span) + jnp.bitwise_xor(core, s // rows)) * rows + s % rows
        here = (place == token) & (lane % span == 0)
        for c in range(CONTROLS):
            at = tokens + (s * CONTROLS + c) * 3
            mask = here & (control == c)
            level = jnp.where(mask, meta[at : at + 1, :], level)
            owner = jnp.where(mask, meta[at + 1 : at + 2, :] + BASE * meta[at + 2 : at + 3, :], owner)
    level = jnp.sum(level, axis=1, keepdims=True)
    owner = jnp.sum(owner, axis=1, keepdims=True).astype(jnp.int32)
    owner = jnp.where(is_base, token[:, :1], owner)
    level = jnp.where(is_base, float(LEVELS), level)
    out = lax.broadcasted_iota(jnp.int32, (tokens, 2 * chips * 8), 1)
    j = out % 8
    chip = (out // 8) % chips
    parity = jnp.bitwise_xor(core, out // (8 * chips))
    base = jnp.where(j < rows, (2 * chip + parity) * rows + j, -1)
    selector = (owner == base).astype(jnp.bfloat16)
    turn = (((0,), (0,)), ((), ()))
    mixed = lax.dot_general(selector, attended, turn, preferred_element_type=jnp.float32).astype(jnp.bfloat16)
    wide = jnp.broadcast_to(level, (tokens, LANES)).astype(jnp.bfloat16)
    weight = lax.dot_general(selector, wide, turn, preferred_element_type=jnp.float32)[:, :1] / LEVELS
    step = 512
    for i in range(w_ref.shape[1] // step):
        at = slice(i * step, (i + 1) * step)
        product = jnp.dot(mixed, w_ref[:, at], preferred_element_type=jnp.float32) * weight
        for c in range(chips):
            mine_ref[c, :, at] = product[8 * c : 8 * c + rows, :].astype(jnp.bfloat16)
            other_ref[c, :, at] = product[8 * (chips + c) : 8 * (chips + c) + rows, :].astype(jnp.bfloat16)


def call(kernel, splits, out_shape, in_specs, scratch, limit, args):
    def body(*refs):
        grouped, at = [], 0
        for size in splits:
            grouped.append(refs[at] if size == 0 else refs[at : at + size])
            at += max(size, 1)
        kernel(*grouped, *refs[at:])

    return pl.pallas_call(
        body,
        out_shape=out_shape,
        in_specs=in_specs,
        out_specs=jax.tree.map(lambda _: VMEM, out_shape),
        scratch_shapes=scratch,
        compiler_params=pltpu.CompilerParams(vmem_limit_bytes=int(limit * 2**20)),
    )(*args)


def on_device(queries, key_rows, value_rows, out_weight, levels, owner_map):
    count = lax.axis_size("seq")
    chips, rows = count // 2, queries.shape[0]
    tokens = rows * count
    heads_dev = out_weight.shape[0] // HD
    width = heads_dev * HD
    keys = key_rows.shape[0]
    extra = -(-2 * heads_dev * tiles_of(tokens, rows) // 8) * 8

    def swap(x, bits):
        return lax.ppermute(x, "seq", [(i, i ^ bits) for i in range(count)])

    there = swap(queries, 1)
    level_there, owner_there = swap(levels, 1), swap(owner_map, 1)
    key_rows, value_rows, there = lax.optimization_barrier((key_rows, value_rows, there))
    rest = [key_rows, swap(key_rows, 1), value_rows, swap(value_rows, 1), levels, level_there, owner_map, owner_there]
    rest = [pltpu.with_memory_space_constraint(x, pltpu.HBM) for x in rest]
    groups = [list(range(c, count, 2)) for c in range(2)]

    def exchange(x):
        return lax.all_to_all(x, "seq", split_axis=0, concat_axis=0, axis_index_groups=groups, tiled=True)

    packed = call(
        functools.partial(pack_kernel, width),
        (),
        jax.ShapeDtypeStruct((GROUPS * 2 * rows, chips * width // GROUPS), jnp.bfloat16),
        [VMEM] * 2,
        [],
        PACK_MIB,
        (queries, there),
    )
    gathered = [pltpu.with_memory_space_constraint(packed, pltpu.HBM)] + [swap(packed, 2 * d) for d in range(1, chips)]
    parts = call(
        functools.partial(attend_kernel, tokens, rows, heads_dev),
        (chips, 2, 2, 2, 2, chips),
        [jax.ShapeDtypeStruct((heads_dev * tokens + extra, HD), jnp.bfloat16)] * chips,
        [VMEM] * chips + [IN_HBM] * 4 + [SMEM] * 4,
        [
            pltpu.VMEM((tokens, chips * width), jnp.bfloat16),
            pltpu.VMEM((2 * keys, chips * width), jnp.bfloat16),
            pltpu.VMEM((2 * keys, chips * width), jnp.bfloat16),
            pltpu.SemaphoreType.DMA((2, 2, chips)),
            pltpu.VMEM((tiles_of(tokens, rows) * LANES, LANES), jnp.float32),
        ],
        ATTEND_MIB,
        (*gathered, *rest),
    )
    share = jax.ShapeDtypeStruct((chips, rows, out_weight.shape[1]), jnp.bfloat16)
    mine, other = call(
        functools.partial(project_kernel, tokens, rows, heads_dev),
        (chips,),
        [share, share],
        [VMEM] * (chips + 1),
        [],
        PROJECT_MIB,
        (parts[0], *(swap(parts[d], 2 * d) for d in range(1, chips)), out_weight),
    )
    summed = exchange((mine.astype(jnp.float32) + swap(other, 1).astype(jnp.float32)).astype(jnp.bfloat16))
    return jnp.sum(summed.astype(jnp.float32), axis=0).astype(jnp.bfloat16)


def solution(mesh):
    return jax.shard_map(
        on_device,
        mesh=mesh,
        in_specs=(
            P(("groups", "seq"), None),
            P(("groups", "seq"), None),
            P(("groups", "seq"), None),
            P("seq", None),
            P(None, ("groups", "seq")),
            P(None, ("groups", "seq")),
        ),
        out_specs=P(("groups", "seq"), None),
        check_vma=False,
    )
```

```python
import functools

import jax
import jax.numpy as jnp
from jax import lax
from jax.experimental import pallas as pl
from jax.experimental.pallas import tpu as pltpu
from jax.sharding import PartitionSpec as P


HD = 128
HEADS = 16
CONTROLS = 3
LEVELS = 8
LANES = 128
BASE = 256
GROUPS = 4
TO_EXP2 = HD ** (-0.5) * 1.4426950408889634

PACK_MIB, ATTEND_MIB, PROJECT_MIB = 8, 24, 16


VMEM = pl.BlockSpec(memory_space=pltpu.VMEM)
SMEM = pl.BlockSpec(memory_space=pltpu.SMEM)
IN_HBM = pl.BlockSpec(memory_space=pltpu.HBM)


def tiles_of(tokens, rows):
    return -(-(tokens + 2 * rows * 3 * CONTROLS) // LANES)


def pack_kernel(width, here_ref, there_ref, out_ref):
    core = lax.rem(lax.axis_index("seq"), 2)
    height, lanes = out_ref.shape
    rows, chips = here_ref.shape[0], here_ref.shape[1] // (2 * width)
    row = lax.broadcasted_iota(jnp.int32, (height, lanes), 0)
    packed = jnp.zeros((height, lanes), jnp.float32)
    for i, q_ref in enumerate((here_ref, there_ref)):
        mine = [
            q_ref[:, pl.ds(pl.multiple_of((2 * chip + core) * width, LANES), width)].astype(jnp.float32)
            for chip in range(chips)
        ]
        mine = jnp.concatenate(mine, axis=1)
        for t in range(rows):
            for g in range(GROUPS):
                packed = jnp.where(
                    row == g * 2 * rows + i * rows + t, mine[t : t + 1, g * lanes : (g + 1) * lanes], packed
                )
    out_ref[...] = packed.astype(jnp.bfloat16)


def attend_kernel(tokens, rows, heads_dev, in_refs, key_refs, value_refs, level_refs, owner_refs, out_refs, q_ref, k_ref, v_ref, sem, stat_ref):
    me = lax.axis_index("seq")
    core, here = lax.rem(me, 2), me // 2
    chips = len(out_refs)
    width = heads_dev * HD
    keys = key_refs[0].shape[0]
    main = heads_dev * tokens

    def block(d):
        return jnp.bitwise_xor(here, d)

    def copies(d):
        at = pl.ds(pl.multiple_of((2 * block(d) + core) * width, LANES), width)
        to = pl.ds(d * width, width)
        for s, refs, buffer in ((0, key_refs, k_ref), (1, value_refs, v_ref)):
            for i, ref in enumerate(refs):
                yield pltpu.make_async_copy(ref.at[:, at], buffer.at[i * keys : (i + 1) * keys, to], sem.at[s, i, d])

    for d in range(chips):
        for copy in copies(d):
            copy.start()

    _, lanes = in_refs[0].shape
    for g in range(GROUPS):
        low, high = g * 2 * rows // 8 * 8, -(-(g + 1) * 2 * rows // 8) * 8
        some = high - low
        gathered = jnp.concatenate([ref[low:high, :] for ref in in_refs], axis=0)
        token = lax.broadcasted_iota(jnp.int32, (tokens, chips * some), 0)
        slot = lax.broadcasted_iota(jnp.int32, (tokens, chips * some), 1)
        at = low + slot % some - g * 2 * rows
        owner_core = jnp.bitwise_xor(core, jnp.where(at >= rows, 1, 0))
        place = (2 * block(slot // some) + owner_core) * rows + jnp.where(at >= rows, at - rows, at)
        pick = ((place == token) & (at >= 0) & (at < 2 * rows)).astype(jnp.bfloat16)
        q_ref[:, g * lanes : (g + 1) * lanes] = jnp.dot(pick, gathered, preferred_element_type=jnp.float32).astype(
            jnp.bfloat16
        )

    lane = lax.broadcasted_iota(jnp.int32, (tokens, LANES), 1)
    stat_ref[...] = jnp.zeros_like(stat_ref)
    stat = jnp.zeros((tokens, LANES), jnp.float32)
    group = 8
    heads = [(d, h) for d in range(chips) for h in range(heads_dev)]
    for first in range(0, len(heads), group):
        some = heads[first : first + group]
        for d in sorted({d for d, _ in some}):
            for copy in copies(d):
                copy.wait()
        scores = []
        for d, h in some:
            columns = slice(d * width + h * HD, d * width + (h + 1) * HD)
            query = q_ref[:, pl.ds(pl.multiple_of(block(d) * width + h * HD, LANES), HD)]
            scores.append(
                lax.dot_general(query, k_ref[:, columns], (((1,), (1,)), ((), ())), preferred_element_type=jnp.float32)
            )
        expo = []
        for (d, h), score in zip(some, scores):
            peak = jnp.max(score, axis=1, keepdims=True).astype(jnp.bfloat16).astype(jnp.float32)
            weights = jnp.exp2((score - peak) * TO_EXP2)
            rowsum = jnp.sum(weights, axis=1, keepdims=True)
            expo.append(weights.astype(jnp.bfloat16))
            at = d * 2 * heads_dev + h
            stat = jnp.where(lane == at, peak, jnp.where(lane == at + heads_dev, rowsum, stat))
        for i in range(0, len(some), 2):
            columns = slice((first + i) * HD, (first + i + 2) * HD)
            product = jnp.dot(jnp.concatenate(expo[i : i + 2], axis=0), v_ref[:, columns], preferred_element_type=jnp.float32)
            for k in range(2):
                d, h = some[i + k]
                out_refs[d][h * tokens : (h + 1) * tokens, :] = product[
                    k * tokens : (k + 1) * tokens, k * HD : (k + 1) * HD
                ].astype(jnp.bfloat16)
    stat_ref[:tokens, :] = stat
    at = tokens
    for level_ref, owner_ref in zip(level_refs, owner_refs):
        for t in range(rows):
            for c in range(CONTROLS):
                owner = owner_ref[c, t]
                for value in (level_ref[c, t], owner & (BASE - 1), owner >> 8):
                    stat_ref[at : at + 1, :] = jnp.full((1, LANES), value, jnp.int32).astype(jnp.float32)
                    at += 1
    span = 2 * heads_dev
    for tile in range(tiles_of(tokens, rows)):
        turned = stat_ref[tile * LANES : (tile + 1) * LANES, :].T.astype(jnp.bfloat16)
        for d in range(chips):
            out_refs[d][main + tile * span : main + (tile + 1) * span, :] = turned[d * span : (d + 1) * span, :]


def project_kernel(tokens, rows, heads_dev, x_refs, w_ref, mine_ref, other_ref):
    me = lax.axis_index("seq")
    core = lax.rem(me, 2)
    chips = len(x_refs)
    main, span = heads_dev * tokens, 2 * heads_dev
    stats, shares = [], []
    for tile in range(tiles_of(tokens, rows)):
        at = main + tile * span
        stat = [x_refs[i][at : at + span, :].astype(jnp.float32) for i in range(chips)]
        stat = jnp.concatenate(stat + [jnp.zeros((LANES - chips * span, LANES), jnp.float32)], axis=0).T
        stats.append(stat)
        stat = jnp.where(lax.broadcasted_iota(jnp.int32, stat.shape, 1) < chips * span, stat, -1e30)
        best, shift = stat, span
        while shift < LANES:
            best = jnp.maximum(best, pltpu.roll(best, shift, 1))
            shift *= 2
        factor = jnp.exp2((stat - best) * TO_EXP2)
        denom, shift = factor * pltpu.roll(stat, LANES - heads_dev, 1), span
        while shift < LANES:
            denom = denom + pltpu.roll(denom, shift, 1)
            shift *= 2
        shares.append(factor / denom)
    share = jnp.concatenate(shares, axis=0)[:tokens, :]
    attended = []
    for h in range(heads_dev):
        total = jnp.zeros((tokens, HD), jnp.float32)
        for i in range(chips):
            at = i * span + h
            total = total + share[:, at : at + 1] * x_refs[i][h * tokens : (h + 1) * tokens, :].astype(jnp.float32)
        attended.append(total.astype(jnp.bfloat16))
    attended = jnp.concatenate(attended, axis=1)

    section = me * heads_dev // HEADS
    control = jnp.minimum(section, CONTROLS - 1)
    is_base = section >= CONTROLS
    meta = jnp.concatenate(stats, axis=0)
    token = lax.broadcasted_iota(jnp.int32, (tokens, LANES), 0)
    lane = lax.broadcasted_iota(jnp.int32, (tokens, LANES), 1)
    level = jnp.zeros((tokens, LANES), jnp.float32)
    owner = jnp.zeros((tokens, LANES), jnp.float32)
    for s in range(2 * rows):
        place = (2 * jnp.bitwise_xor(me // 2, lane // span) + jnp.bitwise_xor(core, s // rows)) * rows + s % rows
        here = (place == token) & (lane % span == 0)
        for c in range(CONTROLS):
            at = tokens + (s * CONTROLS + c) * 3
            mask = here & (control == c)
            level = jnp.where(mask, meta[at : at + 1, :], level)
            owner = jnp.where(mask, meta[at + 1 : at + 2, :] + BASE * meta[at + 2 : at + 3, :], owner)
    level = jnp.sum(level, axis=1, keepdims=True)
    owner = jnp.sum(owner, axis=1, keepdims=True).astype(jnp.int32)
    owner = jnp.where(is_base, token[:, :1], owner)
    level = jnp.where(is_base, float(LEVELS), level)
    out = lax.broadcasted_iota(jnp.int32, (tokens, 2 * chips * 8), 1)
    j = out % 8
    chip = (out // 8) % chips
    parity = jnp.bitwise_xor(core, out // (8 * chips))
    base = jnp.where(j < rows, (2 * chip + parity) * rows + j, -1)
    selector = (owner == base).astype(jnp.bfloat16)
    turn = (((0,), (0,)), ((), ()))
    mixed = lax.dot_general(selector, attended, turn, preferred_element_type=jnp.float32).astype(jnp.bfloat16)
    wide = jnp.broadcast_to(level, (tokens, LANES)).astype(jnp.bfloat16)
    weight = lax.dot_general(selector, wide, turn, preferred_element_type=jnp.float32)[:, :1] / LEVELS
    step = 512
    for i in range(w_ref.shape[1] // step):
        at = slice(i * step, (i + 1) * step)
        product = jnp.dot(mixed, w_ref[:, at], preferred_element_type=jnp.float32) * weight
        for c in range(chips):
            mine_ref[c, :, at] = product[8 * c : 8 * c + rows, :].astype(jnp.bfloat16)
            other_ref[c, :, at] = product[8 * (chips + c) : 8 * (chips + c) + rows, :].astype(jnp.bfloat16)


def call(kernel, splits, out_shape, in_specs, scratch, limit, args):
    def body(*refs):
        grouped, at = [], 0
        for size in splits:
            grouped.append(refs[at] if size == 0 else refs[at : at + size])
            at += max(size, 1)
        kernel(*grouped, *refs[at:])

    return pl.pallas_call(
        body,
        out_shape=out_shape,
        in_specs=in_specs,
        out_specs=jax.tree.map(lambda _: VMEM, out_shape),
        scratch_shapes=scratch,
        compiler_params=pltpu.CompilerParams(vmem_limit_bytes=int(limit * 2**20)),
    )(*args)


def on_device(queries, key_rows, value_rows, out_weight, levels, owner_map):
    count = lax.axis_size("seq")
    chips, rows = count // 2, queries.shape[0]
    tokens = rows * count
    heads_dev = out_weight.shape[0] // HD
    width = heads_dev * HD
    keys = key_rows.shape[0]
    extra = -(-2 * heads_dev * tiles_of(tokens, rows) // 8) * 8

    def swap(x, bits):
        return lax.ppermute(x, "seq", [(i, i ^ bits) for i in range(count)])

    there, level_there, owner_there = swap(queries, 1), swap(levels, 1), swap(owner_map, 1)
    key_there, value_there = swap(key_rows, 1), swap(value_rows, 1)
    rest = [key_rows, key_there, value_rows, value_there, levels, level_there, owner_map, owner_there]
    rest = [x if i in (1, 3) else pltpu.with_memory_space_constraint(x, pltpu.HBM) for i, x in enumerate(rest)]
    groups = [list(range(c, count, 2)) for c in range(2)]

    def exchange(x):
        return lax.all_to_all(x, "seq", split_axis=0, concat_axis=0, axis_index_groups=groups, tiled=True)

    packed = call(
        functools.partial(pack_kernel, width),
        (),
        jax.ShapeDtypeStruct((GROUPS * 2 * rows, chips * width // GROUPS), jnp.bfloat16),
        [VMEM] * 2,
        [],
        PACK_MIB,
        (pltpu.with_memory_space_constraint(queries, pltpu.HBM), there),
    )
    gathered = [packed] + [swap(packed, 2 * d) for d in range(1, chips)]
    parts = call(
        functools.partial(attend_kernel, tokens, rows, heads_dev),
        (chips, 2, 2, 2, 2, chips),
        [jax.ShapeDtypeStruct((heads_dev * tokens + extra, HD), jnp.bfloat16)] * chips,
        [VMEM] * chips + [IN_HBM] * 4 + [SMEM] * 4,
        [
            pltpu.VMEM((tokens, chips * width), jnp.bfloat16),
            pltpu.VMEM((2 * keys, chips * width), jnp.bfloat16),
            pltpu.VMEM((2 * keys, chips * width), jnp.bfloat16),
            pltpu.SemaphoreType.DMA((2, 2, chips)),
            pltpu.VMEM((tiles_of(tokens, rows) * LANES, LANES), jnp.float32),
        ],
        ATTEND_MIB,
        (*gathered, *rest),
    )
    share = jax.ShapeDtypeStruct((chips, rows, out_weight.shape[1]), jnp.bfloat16)
    mine, other = call(
        functools.partial(project_kernel, tokens, rows, heads_dev),
        (chips,),
        [share, share],
        [VMEM] * (chips + 1),
        [],
        PROJECT_MIB,
        (parts[0], *(swap(parts[d], 2 * d) for d in range(1, chips)), out_weight),
    )
    summed = exchange((mine.astype(jnp.float32) + swap(other, 1).astype(jnp.float32)).astype(jnp.bfloat16))
    return jnp.sum(summed.astype(jnp.float32), axis=0).astype(jnp.bfloat16)


def solution(mesh):
    return jax.shard_map(
        on_device,
        mesh=mesh,
        in_specs=(
            P(("groups", "seq"), None),
            P(("groups", "seq"), None),
            P(("groups", "seq"), None),
            P("seq", None),
            P(None, ("groups", "seq")),
            P(None, ("groups", "seq")),
        ),
        out_specs=P(("groups", "seq"), None),
        check_vma=False,
    )
```

```python
import functools

import jax
import jax.numpy as jnp
from jax import lax
from jax.experimental import pallas as pl
from jax.experimental.pallas import tpu as pltpu
from jax.sharding import PartitionSpec as P


HD = 128
HEADS = 16
CONTROLS = 3
LEVELS = 8
LANES = 128
BASE = 256
GROUPS = 4
TO_EXP2 = HD ** (-0.5) * 1.4426950408889634

PACK_MIB, FETCH_MIB, ATTEND_MIB, PROJECT_MIB = 8, 12, 24, 16


VMEM = pl.BlockSpec(memory_space=pltpu.VMEM)
SMEM = pl.BlockSpec(memory_space=pltpu.SMEM)
IN_HBM = pl.BlockSpec(memory_space=pltpu.HBM)


def tiles_of(tokens, rows):
    return -(-(tokens + 2 * rows * 3 * CONTROLS) // LANES)


def pack_kernel(width, here_ref, there_ref, out_ref):
    core = lax.rem(lax.axis_index("seq"), 2)
    height, lanes = out_ref.shape
    rows, chips = here_ref.shape[0], here_ref.shape[1] // (2 * width)
    row = lax.broadcasted_iota(jnp.int32, (height, lanes), 0)
    packed = jnp.zeros((height, lanes), jnp.float32)
    for i, q_ref in enumerate((here_ref, there_ref)):
        mine = [
            q_ref[:, pl.ds(pl.multiple_of((2 * chip + core) * width, LANES), width)].astype(jnp.float32)
            for chip in range(chips)
        ]
        mine = jnp.concatenate(mine, axis=1)
        for t in range(rows):
            for g in range(GROUPS):
                packed = jnp.where(
                    row == g * 2 * rows + i * rows + t, mine[t : t + 1, g * lanes : (g + 1) * lanes], packed
                )
    out_ref[...] = packed.astype(jnp.bfloat16)


def fetch_kernel(chips, in_refs, out_refs, sem):
    me = lax.axis_index("seq")
    core, here = lax.rem(me, 2), me // 2
    width = out_refs[0].shape[1] // chips
    copies = []
    for d in range(chips):
        at = pl.ds(pl.multiple_of((2 * jnp.bitwise_xor(here, d) + core) * width, LANES), width)
        for s in range(2):
            to = out_refs[s].at[:, d * width : (d + 1) * width]
            copies.append(pltpu.make_async_copy(in_refs[s].at[:, at], to, sem.at[s, d]))
    for copy in copies:
        copy.start()
    for copy in copies:
        copy.wait()


def attend_kernel(tokens, rows, heads_dev, in_refs, key_refs, value_refs, level_refs, owner_refs, out_refs, q_ref, stat_ref):
    me = lax.axis_index("seq")
    core, here = lax.rem(me, 2), me // 2
    chips = len(out_refs)
    width = heads_dev * HD
    keys = key_refs[0].shape[0]
    main = heads_dev * tokens

    def block(d):
        return jnp.bitwise_xor(here, d)

    lanes = in_refs[0].shape[1]
    for g in range(GROUPS):
        low, high = g * 2 * rows // 8 * 8, -(-(g + 1) * 2 * rows // 8) * 8
        some = high - low
        gathered = jnp.concatenate([ref[low:high, :] for ref in in_refs], axis=0)
        token = lax.broadcasted_iota(jnp.int32, (tokens, chips * some), 0)
        slot = lax.broadcasted_iota(jnp.int32, (tokens, chips * some), 1)
        at = low + slot % some - g * 2 * rows
        owner_core = jnp.bitwise_xor(core, jnp.where(at >= rows, 1, 0))
        place = (2 * block(slot // some) + owner_core) * rows + jnp.where(at >= rows, at - rows, at)
        pick = ((place == token) & (at >= 0) & (at < 2 * rows)).astype(jnp.bfloat16)
        q_ref[:, g * lanes : (g + 1) * lanes] = jnp.dot(pick, gathered, preferred_element_type=jnp.float32).astype(
            jnp.bfloat16
        )

    lane = lax.broadcasted_iota(jnp.int32, (tokens, LANES), 1)
    stat_ref[...] = jnp.zeros_like(stat_ref)
    stat = jnp.zeros((tokens, LANES), jnp.float32)
    group = 16
    heads = [(d, h) for d in range(chips) for h in range(heads_dev)]
    for first in range(0, len(heads), group):
        some = heads[first : first + group]
        scores = []
        for d, h in some:
            columns = slice(d * width + h * HD, d * width + (h + 1) * HD)
            query = q_ref[:, pl.ds(pl.multiple_of(block(d) * width + h * HD, LANES), HD)]
            there = pl.ds(pl.multiple_of((2 * block(d) + core) * width + h * HD, LANES), HD)
            scores.append(
                jnp.concatenate(
                    [
                        lax.dot_general(query, key, (((1,), (1,)), ((), ())), preferred_element_type=jnp.float32)
                        for key in (key_refs[0][:, columns], key_refs[1][:, there])
                    ],
                    axis=1,
                )
            )
        expo = []
        for (d, h), score in zip(some, scores):
            peak = jnp.max(score, axis=1, keepdims=True).astype(jnp.bfloat16).astype(jnp.float32)
            weights = jnp.exp2((score - peak) * TO_EXP2)
            rowsum = jnp.sum(weights, axis=1, keepdims=True)
            expo.append(weights.astype(jnp.bfloat16))
            at = d * 2 * heads_dev + h
            stat = jnp.where(lane == at, peak, jnp.where(lane == at + heads_dev, rowsum, stat))
        for i in range(0, len(some), 2):
            columns = slice((first + i) * HD, (first + i + 2) * HD)
            weights = jnp.concatenate(expo[i : i + 2], axis=0)
            theirs = [
                value_refs[1][:, pl.ds(pl.multiple_of((2 * block(d) + core) * width + h * HD, LANES), HD)]
                for d, h in some[i : i + 2]
            ]
            product = jnp.dot(weights[:, :keys], value_refs[0][:, columns], preferred_element_type=jnp.float32) + jnp.dot(
                weights[:, keys:], jnp.concatenate(theirs, axis=1), preferred_element_type=jnp.float32
            )
            for k in range(2):
                d, h = some[i + k]
                out_refs[d][h * tokens : (h + 1) * tokens, :] = product[
                    k * tokens : (k + 1) * tokens, k * HD : (k + 1) * HD
                ].astype(jnp.bfloat16)
    stat_ref[:tokens, :] = stat
    at = tokens
    for level_ref, owner_ref in zip(level_refs, owner_refs):
        for t in range(rows):
            for c in range(CONTROLS):
                owner = owner_ref[c, t]
                for value in (level_ref[c, t], owner & (BASE - 1), owner >> 8):
                    stat_ref[at : at + 1, :] = jnp.full((1, LANES), value, jnp.int32).astype(jnp.float32)
                    at += 1
    span = 2 * heads_dev
    for tile in range(tiles_of(tokens, rows)):
        turned = stat_ref[tile * LANES : (tile + 1) * LANES, :].T.astype(jnp.bfloat16)
        for d in range(chips):
            out_refs[d][main + tile * span : main + (tile + 1) * span, :] = turned[d * span : (d + 1) * span, :]


def project_kernel(tokens, rows, heads_dev, x_refs, w_ref, mine_ref, other_ref):
    me = lax.axis_index("seq")
    core = lax.rem(me, 2)
    chips = len(x_refs)
    main, span = heads_dev * tokens, 2 * heads_dev
    stats, shares = [], []
    for tile in range(tiles_of(tokens, rows)):
        at = main + tile * span
        stat = [x_refs[i][at : at + span, :].astype(jnp.float32) for i in range(chips)]
        stat = jnp.concatenate(stat + [jnp.zeros((LANES - chips * span, LANES), jnp.float32)], axis=0).T
        stats.append(stat)
        stat = jnp.where(lax.broadcasted_iota(jnp.int32, stat.shape, 1) < chips * span, stat, -1e30)
        best, shift = stat, span
        while shift < LANES:
            best = jnp.maximum(best, pltpu.roll(best, shift, 1))
            shift *= 2
        factor = jnp.exp2((stat - best) * TO_EXP2)
        denom, shift = factor * pltpu.roll(stat, LANES - heads_dev, 1), span
        while shift < LANES:
            denom = denom + pltpu.roll(denom, shift, 1)
            shift *= 2
        shares.append(factor / denom)
    share = jnp.concatenate(shares, axis=0)[:tokens, :]
    attended = []
    for h in range(heads_dev):
        total = jnp.zeros((tokens, HD), jnp.float32)
        for i in range(chips):
            at = i * span + h
            total = total + share[:, at : at + 1] * x_refs[i][h * tokens : (h + 1) * tokens, :].astype(jnp.float32)
        attended.append(total.astype(jnp.bfloat16))
    attended = jnp.concatenate(attended, axis=1)

    section = me * heads_dev // HEADS
    control = jnp.minimum(section, CONTROLS - 1)
    is_base = section >= CONTROLS
    meta = jnp.concatenate(stats, axis=0)
    token = lax.broadcasted_iota(jnp.int32, (tokens, LANES), 0)
    lane = lax.broadcasted_iota(jnp.int32, (tokens, LANES), 1)
    level = jnp.zeros((tokens, LANES), jnp.float32)
    owner = jnp.zeros((tokens, LANES), jnp.float32)
    for s in range(2 * rows):
        place = (2 * jnp.bitwise_xor(me // 2, lane // span) + jnp.bitwise_xor(core, s // rows)) * rows + s % rows
        here = (place == token) & (lane % span == 0)
        for c in range(CONTROLS):
            at = tokens + (s * CONTROLS + c) * 3
            mask = here & (control == c)
            level = jnp.where(mask, meta[at : at + 1, :], level)
            owner = jnp.where(mask, meta[at + 1 : at + 2, :] + BASE * meta[at + 2 : at + 3, :], owner)
    level = jnp.sum(level, axis=1, keepdims=True)
    owner = jnp.sum(owner, axis=1, keepdims=True).astype(jnp.int32)
    owner = jnp.where(is_base, token[:, :1], owner)
    level = jnp.where(is_base, float(LEVELS), level)
    out = lax.broadcasted_iota(jnp.int32, (tokens, 2 * chips * 8), 1)
    j = out % 8
    chip = (out // 8) % chips
    parity = jnp.bitwise_xor(core, out // (8 * chips))
    base = jnp.where(j < rows, (2 * chip + parity) * rows + j, -1)
    selector = (owner == base).astype(jnp.bfloat16)
    turn = (((0,), (0,)), ((), ()))
    mixed = lax.dot_general(selector, attended, turn, preferred_element_type=jnp.float32).astype(jnp.bfloat16)
    wide = jnp.broadcast_to(level, (tokens, LANES)).astype(jnp.bfloat16)
    weight = lax.dot_general(selector, wide, turn, preferred_element_type=jnp.float32)[:, :1] / LEVELS
    step = 512
    for i in range(w_ref.shape[1] // step):
        at = slice(i * step, (i + 1) * step)
        product = jnp.dot(mixed, w_ref[:, at], preferred_element_type=jnp.float32) * weight
        for c in range(chips):
            mine_ref[c, :, at] = product[8 * c : 8 * c + rows, :].astype(jnp.bfloat16)
            other_ref[c, :, at] = product[8 * (chips + c) : 8 * (chips + c) + rows, :].astype(jnp.bfloat16)


def call(kernel, splits, out_shape, in_specs, scratch, limit, args):
    def body(*refs):
        grouped, at = [], 0
        for size in splits:
            grouped.append(refs[at] if size == 0 else refs[at : at + size])
            at += max(size, 1)
        kernel(*grouped, *refs[at:])

    return pl.pallas_call(
        body,
        out_shape=out_shape,
        in_specs=in_specs,
        out_specs=jax.tree.map(lambda _: VMEM, out_shape),
        scratch_shapes=scratch,
        compiler_params=pltpu.CompilerParams(vmem_limit_bytes=int(limit * 2**20)),
    )(*args)


def on_device(queries, key_rows, value_rows, out_weight, levels, owner_map):
    count = lax.axis_size("seq")
    chips, rows = count // 2, queries.shape[0]
    tokens = rows * count
    heads_dev = out_weight.shape[0] // HD
    width = heads_dev * HD
    keys = key_rows.shape[0]
    extra = -(-2 * heads_dev * tiles_of(tokens, rows) // 8) * 8

    def swap(x, bits):
        return lax.ppermute(x, "seq", [(i, i ^ bits) for i in range(count)])

    there, level_there, owner_there = swap(queries, 1), swap(levels, 1), swap(owner_map, 1)
    key_there, value_there = swap(key_rows, 1), swap(value_rows, 1)
    own = jax.ShapeDtypeStruct((keys, chips * width), key_rows.dtype)
    key_here, value_here = call(
        functools.partial(fetch_kernel, chips),
        (2, 2),
        [own] * 2,
        [IN_HBM] * 2,
        [pltpu.SemaphoreType.DMA((2, chips))],
        FETCH_MIB,
        tuple(pltpu.with_memory_space_constraint(x, pltpu.HBM) for x in (key_rows, value_rows)),
    )
    rest = [key_here, key_there, value_here, value_there]
    rest += [pltpu.with_memory_space_constraint(x, pltpu.HBM) for x in (levels, level_there, owner_map, owner_there)]
    groups = [list(range(c, count, 2)) for c in range(2)]

    def exchange(x):
        return lax.all_to_all(x, "seq", split_axis=0, concat_axis=0, axis_index_groups=groups, tiled=True)

    packed = call(
        functools.partial(pack_kernel, width),
        (),
        jax.ShapeDtypeStruct((GROUPS * 2 * rows, chips * width // GROUPS), jnp.bfloat16),
        [VMEM] * 2,
        [],
        PACK_MIB,
        (pltpu.with_memory_space_constraint(queries, pltpu.HBM), there),
    )
    gathered = [packed] + [swap(packed, 2 * d) for d in range(1, chips)]
    parts = call(
        functools.partial(attend_kernel, tokens, rows, heads_dev),
        (chips, 2, 2, 2, 2, chips),
        [jax.ShapeDtypeStruct((heads_dev * tokens + extra, HD), jnp.bfloat16)] * chips,
        [VMEM] * (chips + 4) + [SMEM] * 4,
        [
            pltpu.VMEM((tokens, chips * width), jnp.bfloat16),
            pltpu.VMEM((tiles_of(tokens, rows) * LANES, LANES), jnp.float32),
        ],
        ATTEND_MIB,
        (*gathered, *rest),
    )
    share = jax.ShapeDtypeStruct((chips, rows, out_weight.shape[1]), jnp.bfloat16)
    mine, other = call(
        functools.partial(project_kernel, tokens, rows, heads_dev),
        (chips,),
        [share, share],
        [VMEM] * (chips + 1),
        [],
        PROJECT_MIB,
        (parts[0], *(swap(parts[d], 2 * d) for d in range(1, chips)), out_weight),
    )
    summed = exchange((mine.astype(jnp.float32) + swap(other, 1).astype(jnp.float32)).astype(jnp.bfloat16))
    return jnp.sum(summed.astype(jnp.float32), axis=0).astype(jnp.bfloat16)


def solution(mesh):
    return jax.shard_map(
        on_device,
        mesh=mesh,
        in_specs=(
            P(("groups", "seq"), None),
            P(("groups", "seq"), None),
            P(("groups", "seq"), None),
            P("seq", None),
            P(None, ("groups", "seq")),
            P(None, ("groups", "seq")),
        ),
        out_specs=P(("groups", "seq"), None),
        check_vma=False,
    )
```

```python
import functools

import jax
import jax.numpy as jnp
from jax import lax
from jax.experimental import pallas as pl
from jax.experimental.pallas import tpu as pltpu
from jax.sharding import PartitionSpec as P


HD = 128
HEADS = 16
CONTROLS = 3
LEVELS = 8
LANES = 128
BASE = 256
GROUPS = 4
BLOCK = 512
TO_EXP2 = HD ** (-0.5) * 1.4426950408889634

PACK_MIB, FETCH_MIB, ATTEND_MIB, PROJECT_MIB = 8, 12, 24, 16


VMEM = pl.BlockSpec(memory_space=pltpu.VMEM)
SMEM = pl.BlockSpec(memory_space=pltpu.SMEM)
IN_HBM = pl.BlockSpec(memory_space=pltpu.HBM)


def tiles_of(tokens, rows):
    return -(-(tokens + 2 * rows * 3 * CONTROLS) // LANES)


def pack_kernel(width, here_ref, there_ref, out_ref):
    core = lax.rem(lax.axis_index("seq"), 2)
    height, lanes = out_ref.shape
    rows, chips = here_ref.shape[0], here_ref.shape[1] // (2 * width)
    row = lax.broadcasted_iota(jnp.int32, (height, lanes), 0)
    packed = jnp.zeros((height, lanes), jnp.float32)
    for i, q_ref in enumerate((here_ref, there_ref)):
        mine = [
            q_ref[:, pl.ds(pl.multiple_of((2 * chip + core) * width, LANES), width)].astype(jnp.float32)
            for chip in range(chips)
        ]
        mine = jnp.concatenate(mine, axis=1)
        for t in range(rows):
            for g in range(GROUPS):
                packed = jnp.where(
                    row == g * 2 * rows + i * rows + t, mine[t : t + 1, g * lanes : (g + 1) * lanes], packed
                )
    out_ref[...] = packed.astype(jnp.bfloat16)


def fetch_kernel(chips, in_refs, out_refs, sem):
    me = lax.axis_index("seq")
    core, here = lax.rem(me, 2), me // 2
    width = out_refs[0].shape[1] // chips
    copies = []
    for d in range(chips):
        at = pl.ds(pl.multiple_of((2 * jnp.bitwise_xor(here, d) + core) * width, LANES), width)
        for s in range(2):
            to = out_refs[s].at[:, d * width : (d + 1) * width]
            copies.append(pltpu.make_async_copy(in_refs[s].at[:, at], to, sem.at[s, d]))
    for copy in copies:
        copy.start()
    for copy in copies:
        copy.wait()


def attend_kernel(tokens, rows, heads_dev, in_refs, key_refs, value_refs, level_refs, owner_refs, out_refs, q_ref, stat_ref):
    me = lax.axis_index("seq")
    core, here = lax.rem(me, 2), me // 2
    chips = len(out_refs)
    width = heads_dev * HD
    keys = key_refs[0].shape[0]
    main = heads_dev * tokens

    def block(d):
        return jnp.bitwise_xor(here, d)

    lanes = in_refs[0].shape[1]
    for g in range(GROUPS):
        low, high = g * 2 * rows // 8 * 8, -(-(g + 1) * 2 * rows // 8) * 8
        some = high - low
        gathered = jnp.concatenate([ref[low:high, :] for ref in in_refs], axis=0)
        token = lax.broadcasted_iota(jnp.int32, (tokens, chips * some), 0)
        slot = lax.broadcasted_iota(jnp.int32, (tokens, chips * some), 1)
        at = low + slot % some - g * 2 * rows
        owner_core = jnp.bitwise_xor(core, jnp.where(at >= rows, 1, 0))
        place = (2 * block(slot // some) + owner_core) * rows + jnp.where(at >= rows, at - rows, at)
        pick = ((place == token) & (at >= 0) & (at < 2 * rows)).astype(jnp.bfloat16)
        q_ref[:, g * lanes : (g + 1) * lanes] = jnp.dot(pick, gathered, preferred_element_type=jnp.float32).astype(
            jnp.bfloat16
        )

    lane = lax.broadcasted_iota(jnp.int32, (tokens, LANES), 1)
    stat_ref[...] = jnp.zeros_like(stat_ref)
    stat = jnp.zeros((tokens, LANES), jnp.float32)
    group = 16
    heads = [(d, h) for d in range(chips) for h in range(heads_dev)]
    for first in range(0, len(heads), group):
        some = heads[first : first + group]
        scores = []
        for d, h in some:
            columns = slice(d * width + h * HD, d * width + (h + 1) * HD)
            query = q_ref[:, pl.ds(pl.multiple_of(block(d) * width + h * HD, LANES), HD)]
            there = pl.ds(pl.multiple_of((2 * block(d) + core) * width + h * HD, LANES), HD)
            scores.append(
                jnp.concatenate(
                    [
                        lax.dot_general(query, key, (((1,), (1,)), ((), ())), preferred_element_type=jnp.float32)
                        for key in (key_refs[0][:, columns], key_refs[1][:, there])
                    ],
                    axis=1,
                )
            )
        expo = []
        for (d, h), score in zip(some, scores):
            peak = jnp.max(score, axis=1, keepdims=True).astype(jnp.bfloat16).astype(jnp.float32)
            weights = jnp.exp2((score - peak) * TO_EXP2)
            rowsum = jnp.sum(weights, axis=1, keepdims=True)
            expo.append(weights.astype(jnp.bfloat16))
            at = d * 2 * heads_dev + h
            stat = jnp.where(lane == at, peak, jnp.where(lane == at + heads_dev, rowsum, stat))
        for i in range(0, len(some), 2):
            columns = slice((first + i) * HD, (first + i + 2) * HD)
            weights = jnp.concatenate(expo[i : i + 2], axis=0)
            theirs = [
                value_refs[1][:, pl.ds(pl.multiple_of((2 * block(d) + core) * width + h * HD, LANES), HD)]
                for d, h in some[i : i + 2]
            ]
            product = jnp.dot(weights[:, :keys], value_refs[0][:, columns], preferred_element_type=jnp.float32) + jnp.dot(
                weights[:, keys:], jnp.concatenate(theirs, axis=1), preferred_element_type=jnp.float32
            )
            for k in range(2):
                d, h = some[i + k]
                out_refs[d][h * tokens : (h + 1) * tokens, :] = product[
                    k * tokens : (k + 1) * tokens, k * HD : (k + 1) * HD
                ].astype(jnp.bfloat16)
    stat_ref[:tokens, :] = stat
    at = tokens
    for level_ref, owner_ref in zip(level_refs, owner_refs):
        for t in range(rows):
            for c in range(CONTROLS):
                owner = owner_ref[c, t]
                for value in (level_ref[c, t], owner & (BASE - 1), owner >> 8):
                    stat_ref[at : at + 1, :] = jnp.full((1, LANES), value, jnp.int32).astype(jnp.float32)
                    at += 1
    span = 2 * heads_dev
    for tile in range(tiles_of(tokens, rows)):
        turned = stat_ref[tile * LANES : (tile + 1) * LANES, :].T.astype(jnp.bfloat16)
        for d in range(chips):
            out_refs[d][main + tile * span : main + (tile + 1) * span, :] = turned[d * span : (d + 1) * span, :]


def project_kernel(tokens, rows, heads_dev, x_refs, w_ref, mine_ref, other_ref):
    me = lax.axis_index("seq")
    core = lax.rem(me, 2)
    chips = len(x_refs)
    main, span = heads_dev * tokens, 2 * heads_dev
    stats, shares = [], []
    for tile in range(tiles_of(tokens, rows)):
        at = main + tile * span
        stat = [x_refs[i][at : at + span, :].astype(jnp.float32) for i in range(chips)]
        stat = jnp.concatenate(stat + [jnp.zeros((LANES - chips * span, LANES), jnp.float32)], axis=0).T
        stats.append(stat)
        stat = jnp.where(lax.broadcasted_iota(jnp.int32, stat.shape, 1) < chips * span, stat, -1e30)
        best, shift = stat, span
        while shift < LANES:
            best = jnp.maximum(best, pltpu.roll(best, shift, 1))
            shift *= 2
        factor = jnp.exp2((stat - best) * TO_EXP2)
        denom, shift = factor * pltpu.roll(stat, LANES - heads_dev, 1), span
        while shift < LANES:
            denom = denom + pltpu.roll(denom, shift, 1)
            shift *= 2
        shares.append(factor / denom)
    share = jnp.concatenate(shares, axis=0)[:tokens, :]
    attended = []
    for h in range(heads_dev):
        total = jnp.zeros((tokens, HD), jnp.float32)
        for i in range(chips):
            at = i * span + h
            total = total + share[:, at : at + 1] * x_refs[i][h * tokens : (h + 1) * tokens, :].astype(jnp.float32)
        attended.append(total.astype(jnp.bfloat16))
    attended = jnp.concatenate(attended, axis=1)

    section = me * heads_dev // HEADS
    control = jnp.minimum(section, CONTROLS - 1)
    is_base = section >= CONTROLS
    meta = jnp.concatenate(stats, axis=0)
    token = lax.broadcasted_iota(jnp.int32, (tokens, LANES), 0)
    lane = lax.broadcasted_iota(jnp.int32, (tokens, LANES), 1)
    level = jnp.zeros((tokens, LANES), jnp.float32)
    owner = jnp.zeros((tokens, LANES), jnp.float32)
    for s in range(2 * rows):
        place = (2 * jnp.bitwise_xor(me // 2, lane // span) + jnp.bitwise_xor(core, s // rows)) * rows + s % rows
        here = (place == token) & (lane % span == 0)
        for c in range(CONTROLS):
            at = tokens + (s * CONTROLS + c) * 3
            mask = here & (control == c)
            level = jnp.where(mask, meta[at : at + 1, :], level)
            owner = jnp.where(mask, meta[at + 1 : at + 2, :] + BASE * meta[at + 2 : at + 3, :], owner)
    level = jnp.sum(level, axis=1, keepdims=True)
    owner = jnp.sum(owner, axis=1, keepdims=True).astype(jnp.int32)
    owner = jnp.where(is_base, token[:, :1], owner)
    level = jnp.where(is_base, float(LEVELS), level)
    out = lax.broadcasted_iota(jnp.int32, (tokens, 2 * chips * 8), 1)
    j = out % 8
    chip = (out // 8) % chips
    parity = jnp.bitwise_xor(core, out // (8 * chips))
    base = jnp.where(j < rows, (2 * chip + parity) * rows + j, -1)
    selector = (owner == base).astype(jnp.bfloat16)
    turn = (((0,), (0,)), ((), ()))
    mixed = lax.dot_general(selector, attended, turn, preferred_element_type=jnp.float32).astype(jnp.bfloat16)
    wide = jnp.broadcast_to(level, (tokens, LANES)).astype(jnp.bfloat16)
    weight = lax.dot_general(selector, wide, turn, preferred_element_type=jnp.float32)[:, :1] / LEVELS
    step = mine_ref.shape[2]
    for i in range(w_ref.shape[1] // step):
        to = slice(i * rows, (i + 1) * rows)
        at = slice(i * step, (i + 1) * step)
        product = jnp.dot(mixed, w_ref[:, at], preferred_element_type=jnp.float32) * weight
        for c in range(chips):
            mine_ref[c, to, :] = product[8 * c : 8 * c + rows, :].astype(jnp.bfloat16)
            other_ref[c, to, :] = product[8 * (chips + c) : 8 * (chips + c) + rows, :].astype(jnp.bfloat16)


def total_kernel(x_ref, out_ref):
    total = jnp.sum(x_ref[...].astype(jnp.float32), axis=0)
    rows, step = out_ref.shape[0], x_ref.shape[2]
    for i in range(out_ref.shape[1] // step):
        out_ref[:, i * step : (i + 1) * step] = total[i * rows : (i + 1) * rows, :].astype(jnp.bfloat16)


def call(kernel, splits, out_shape, in_specs, scratch, limit, args):
    def body(*refs):
        grouped, at = [], 0
        for size in splits:
            grouped.append(refs[at] if size == 0 else refs[at : at + size])
            at += max(size, 1)
        kernel(*grouped, *refs[at:])

    return pl.pallas_call(
        body,
        out_shape=out_shape,
        in_specs=in_specs,
        out_specs=jax.tree.map(lambda _: VMEM, out_shape),
        scratch_shapes=scratch,
        compiler_params=pltpu.CompilerParams(vmem_limit_bytes=int(limit * 2**20)),
    )(*args)


def on_device(queries, key_rows, value_rows, out_weight, levels, owner_map):
    count = lax.axis_size("seq")
    chips, rows = count // 2, queries.shape[0]
    tokens = rows * count
    heads_dev = out_weight.shape[0] // HD
    width = heads_dev * HD
    keys = key_rows.shape[0]
    extra = -(-2 * heads_dev * tiles_of(tokens, rows) // 8) * 8

    def swap(x, bits):
        return lax.ppermute(x, "seq", [(i, i ^ bits) for i in range(count)])

    there, level_there, owner_there = swap(queries, 1), swap(levels, 1), swap(owner_map, 1)
    key_there, value_there = swap(key_rows, 1), swap(value_rows, 1)
    own = jax.ShapeDtypeStruct((keys, chips * width), key_rows.dtype)
    key_here, value_here = call(
        functools.partial(fetch_kernel, chips),
        (2, 2),
        [own] * 2,
        [IN_HBM] * 2,
        [pltpu.SemaphoreType.DMA((2, chips))],
        FETCH_MIB,
        tuple(pltpu.with_memory_space_constraint(x, pltpu.HBM) for x in (key_rows, value_rows)),
    )
    rest = [key_here, key_there, value_here, value_there]
    rest += [pltpu.with_memory_space_constraint(x, pltpu.HBM) for x in (levels, level_there, owner_map, owner_there)]
    groups = [list(range(c, count, 2)) for c in range(2)]

    def exchange(x):
        return lax.all_to_all(x, "seq", split_axis=0, concat_axis=0, axis_index_groups=groups, tiled=True)

    packed = call(
        functools.partial(pack_kernel, width),
        (),
        jax.ShapeDtypeStruct((GROUPS * 2 * rows, chips * width // GROUPS), jnp.bfloat16),
        [VMEM] * 2,
        [],
        PACK_MIB,
        (pltpu.with_memory_space_constraint(queries, pltpu.HBM), there),
    )
    gathered = [packed] + [swap(packed, 2 * d) for d in range(1, chips)]
    parts = call(
        functools.partial(attend_kernel, tokens, rows, heads_dev),
        (chips, 2, 2, 2, 2, chips),
        [jax.ShapeDtypeStruct((heads_dev * tokens + extra, HD), jnp.bfloat16)] * chips,
        [VMEM] * (chips + 4) + [SMEM] * 4,
        [
            pltpu.VMEM((tokens, chips * width), jnp.bfloat16),
            pltpu.VMEM((tiles_of(tokens, rows) * LANES, LANES), jnp.float32),
        ],
        ATTEND_MIB,
        (*gathered, *rest),
    )
    columns = out_weight.shape[1]
    share = jax.ShapeDtypeStruct((chips, rows * columns // BLOCK, BLOCK), jnp.bfloat16)
    mine, other = call(
        functools.partial(project_kernel, tokens, rows, heads_dev),
        (chips,),
        [share, share],
        [VMEM] * (chips + 1),
        [],
        PROJECT_MIB,
        (parts[0], *(swap(parts[d], 2 * d) for d in range(1, chips)), out_weight),
    )
    summed = exchange((mine.astype(jnp.float32) + swap(other, 1).astype(jnp.float32)).astype(jnp.bfloat16))
    return call(total_kernel, (), jax.ShapeDtypeStruct((rows, columns), jnp.bfloat16), [VMEM], [], 8, (summed,))


def solution(mesh):
    return jax.shard_map(
        on_device,
        mesh=mesh,
        in_specs=(
            P(("groups", "seq"), None),
            P(("groups", "seq"), None),
            P(("groups", "seq"), None),
            P("seq", None),
            P(None, ("groups", "seq")),
            P(None, ("groups", "seq")),
        ),
        out_specs=P(("groups", "seq"), None),
        check_vma=False,
    )
```

```python
import functools

import jax
import jax.numpy as jnp
from jax import lax
from jax.experimental import pallas as pl
from jax.experimental.pallas import tpu as pltpu
from jax.sharding import PartitionSpec as P


HD = 128
HEADS = 16
CONTROLS = 3
LEVELS = 8
LANES = 128
BASE = 256
GROUPS = 4
BLOCK = 512
TO_EXP2 = HD ** (-0.5) * 1.4426950408889634

PACK_MIB, FETCH_MIB, ATTEND_MIB, PROJECT_MIB = 8, 12, 24, 16


VMEM = pl.BlockSpec(memory_space=pltpu.VMEM)
SMEM = pl.BlockSpec(memory_space=pltpu.SMEM)
IN_HBM = pl.BlockSpec(memory_space=pltpu.HBM)


def tiles_of(tokens, rows):
    return -(-(tokens + 2 * rows * 3 * CONTROLS) // LANES)


def pack_kernel(width, here_ref, there_ref, out_ref):
    core = lax.rem(lax.axis_index("seq"), 2)
    height, lanes = out_ref.shape
    rows, chips = here_ref.shape[0], here_ref.shape[1] // (2 * width)
    row = lax.broadcasted_iota(jnp.int32, (height, lanes), 0)
    packed = jnp.zeros((height, lanes), jnp.float32)
    for i, q_ref in enumerate((here_ref, there_ref)):
        mine = [
            q_ref[:, pl.ds(pl.multiple_of((2 * chip + core) * width, LANES), width)].astype(jnp.float32)
            for chip in range(chips)
        ]
        mine = jnp.concatenate(mine, axis=1)
        for t in range(rows):
            for g in range(GROUPS):
                packed = jnp.where(
                    row == g * 2 * rows + i * rows + t, mine[t : t + 1, g * lanes : (g + 1) * lanes], packed
                )
    out_ref[...] = packed.astype(jnp.bfloat16)


def fetch_kernel(chips, in_refs, out_refs, sem):
    me = lax.axis_index("seq")
    core, here = lax.rem(me, 2), me // 2
    width = out_refs[0].shape[1] // chips
    copies = []
    for d in range(chips):
        at = pl.ds(pl.multiple_of((2 * jnp.bitwise_xor(here, d) + core) * width, LANES), width)
        for s in range(2):
            to = out_refs[s].at[:, d * width : (d + 1) * width]
            copies.append(pltpu.make_async_copy(in_refs[s].at[:, at], to, sem.at[s, d]))
    for copy in copies:
        copy.start()
    for copy in copies:
        copy.wait()


def attend_kernel(tokens, rows, heads_dev, in_refs, key_refs, value_refs, level_refs, owner_refs, out_refs, q_ref, stat_ref):
    me = lax.axis_index("seq")
    core, here = lax.rem(me, 2), me // 2
    chips = len(out_refs)
    width = heads_dev * HD
    keys = key_refs[0].shape[0]
    main = heads_dev * tokens

    def block(d):
        return jnp.bitwise_xor(here, d)

    lanes = in_refs[0].shape[1]
    for g in range(GROUPS):
        low, high = g * 2 * rows // 8 * 8, -(-(g + 1) * 2 * rows // 8) * 8
        some = high - low
        gathered = jnp.concatenate([ref[low:high, :] for ref in in_refs], axis=0)
        token = lax.broadcasted_iota(jnp.int32, (tokens, chips * some), 0)
        slot = lax.broadcasted_iota(jnp.int32, (tokens, chips * some), 1)
        at = low + slot % some - g * 2 * rows
        owner_core = jnp.bitwise_xor(core, jnp.where(at >= rows, 1, 0))
        place = (2 * block(slot // some) + owner_core) * rows + jnp.where(at >= rows, at - rows, at)
        pick = ((place == token) & (at >= 0) & (at < 2 * rows)).astype(jnp.bfloat16)
        q_ref[:, g * lanes : (g + 1) * lanes] = jnp.dot(pick, gathered, preferred_element_type=jnp.float32).astype(
            jnp.bfloat16
        )

    lane = lax.broadcasted_iota(jnp.int32, (tokens, LANES), 1)
    stat_ref[...] = jnp.zeros_like(stat_ref)
    stat = jnp.zeros((tokens, LANES), jnp.float32)
    group = 32
    heads = [(d, h) for d in range(chips) for h in range(heads_dev)]
    for first in range(0, len(heads), group):
        some = heads[first : first + group]
        scores = []
        for d, h in some:
            columns = slice(d * width + h * HD, d * width + (h + 1) * HD)
            query = q_ref[:, pl.ds(pl.multiple_of(block(d) * width + h * HD, LANES), HD)]
            there = pl.ds(pl.multiple_of((2 * block(d) + core) * width + h * HD, LANES), HD)
            scores.append(
                jnp.concatenate(
                    [
                        lax.dot_general(query, key, (((1,), (1,)), ((), ())), preferred_element_type=jnp.float32)
                        for key in (key_refs[0][:, columns], key_refs[1][:, there])
                    ],
                    axis=1,
                )
            )
        expo = []
        for (d, h), score in zip(some, scores):
            peak = jnp.max(score, axis=1, keepdims=True).astype(jnp.bfloat16).astype(jnp.float32)
            weights = jnp.exp2((score - peak) * TO_EXP2)
            rowsum = jnp.sum(weights, axis=1, keepdims=True)
            expo.append(weights.astype(jnp.bfloat16))
            at = d * 2 * heads_dev + h
            stat = jnp.where(lane == at, peak, jnp.where(lane == at + heads_dev, rowsum, stat))
        for i in range(0, len(some), 2):
            columns = slice((first + i) * HD, (first + i + 2) * HD)
            weights = jnp.concatenate(expo[i : i + 2], axis=0)
            theirs = [
                value_refs[1][:, pl.ds(pl.multiple_of((2 * block(d) + core) * width + h * HD, LANES), HD)]
                for d, h in some[i : i + 2]
            ]
            product = jnp.dot(weights[:, :keys], value_refs[0][:, columns], preferred_element_type=jnp.float32) + jnp.dot(
                weights[:, keys:], jnp.concatenate(theirs, axis=1), preferred_element_type=jnp.float32
            )
            for k in range(2):
                d, h = some[i + k]
                out_refs[d][h * tokens : (h + 1) * tokens, :] = product[
                    k * tokens : (k + 1) * tokens, k * HD : (k + 1) * HD
                ].astype(jnp.bfloat16)
    stat_ref[:tokens, :] = stat
    at = tokens
    for level_ref, owner_ref in zip(level_refs, owner_refs):
        for t in range(rows):
            for c in range(CONTROLS):
                owner = owner_ref[c, t]
                for value in (level_ref[c, t], owner & (BASE - 1), owner >> 8):
                    stat_ref[at : at + 1, :] = jnp.full((1, LANES), value, jnp.int32).astype(jnp.float32)
                    at += 1
    span = 2 * heads_dev
    for tile in range(tiles_of(tokens, rows)):
        turned = stat_ref[tile * LANES : (tile + 1) * LANES, :].T.astype(jnp.bfloat16)
        for d in range(chips):
            out_refs[d][main + tile * span : main + (tile + 1) * span, :] = turned[d * span : (d + 1) * span, :]


def project_kernel(tokens, rows, heads_dev, x_refs, w_ref, mine_ref, other_ref):
    me = lax.axis_index("seq")
    core = lax.rem(me, 2)
    chips = len(x_refs)
    main, span = heads_dev * tokens, 2 * heads_dev
    stats, shares = [], []
    for tile in range(tiles_of(tokens, rows)):
        at = main + tile * span
        stat = [x_refs[i][at : at + span, :].astype(jnp.float32) for i in range(chips)]
        stat = jnp.concatenate(stat + [jnp.zeros((LANES - chips * span, LANES), jnp.float32)], axis=0).T
        stats.append(stat)
        stat = jnp.where(lax.broadcasted_iota(jnp.int32, stat.shape, 1) < chips * span, stat, -1e30)
        best, shift = stat, span
        while shift < LANES:
            best = jnp.maximum(best, pltpu.roll(best, shift, 1))
            shift *= 2
        factor = jnp.exp2((stat - best) * TO_EXP2)
        denom, shift = factor * pltpu.roll(stat, LANES - heads_dev, 1), span
        while shift < LANES:
            denom = denom + pltpu.roll(denom, shift, 1)
            shift *= 2
        shares.append(factor / denom)
    share = jnp.concatenate(shares, axis=0)[:tokens, :]
    attended = []
    for h in range(heads_dev):
        total = jnp.zeros((tokens, HD), jnp.float32)
        for i in range(chips):
            at = i * span + h
            total = total + share[:, at : at + 1] * x_refs[i][h * tokens : (h + 1) * tokens, :].astype(jnp.float32)
        attended.append(total.astype(jnp.bfloat16))
    attended = jnp.concatenate(attended, axis=1)

    section = me * heads_dev // HEADS
    control = jnp.minimum(section, CONTROLS - 1)
    is_base = section >= CONTROLS
    meta = jnp.concatenate(stats, axis=0)
    token = lax.broadcasted_iota(jnp.int32, (tokens, LANES), 0)
    lane = lax.broadcasted_iota(jnp.int32, (tokens, LANES), 1)
    level = jnp.zeros((tokens, LANES), jnp.float32)
    owner = jnp.zeros((tokens, LANES), jnp.float32)
    for s in range(2 * rows):
        place = (2 * jnp.bitwise_xor(me // 2, lane // span) + jnp.bitwise_xor(core, s // rows)) * rows + s % rows
        here = (place == token) & (lane % span == 0)
        for c in range(CONTROLS):
            at = tokens + (s * CONTROLS + c) * 3
            mask = here & (control == c)
            level = jnp.where(mask, meta[at : at + 1, :], level)
            owner = jnp.where(mask, meta[at + 1 : at + 2, :] + BASE * meta[at + 2 : at + 3, :], owner)
    level = jnp.sum(level, axis=1, keepdims=True)
    owner = jnp.sum(owner, axis=1, keepdims=True).astype(jnp.int32)
    owner = jnp.where(is_base, token[:, :1], owner)
    level = jnp.where(is_base, float(LEVELS), level)
    out = lax.broadcasted_iota(jnp.int32, (tokens, 2 * chips * 8), 1)
    j = out % 8
    chip = (out // 8) % chips
    parity = jnp.bitwise_xor(core, out // (8 * chips))
    base = jnp.where(j < rows, (2 * chip + parity) * rows + j, -1)
    selector = (owner == base).astype(jnp.bfloat16)
    turn = (((0,), (0,)), ((), ()))
    mixed = lax.dot_general(selector, attended, turn, preferred_element_type=jnp.float32).astype(jnp.bfloat16)
    wide = jnp.broadcast_to(level, (tokens, LANES)).astype(jnp.bfloat16)
    weight = lax.dot_general(selector, wide, turn, preferred_element_type=jnp.float32)[:, :1] / LEVELS
    step = mine_ref.shape[2]
    for i in range(0, w_ref.shape[1] // step, 2):
        wide = jnp.dot(mixed, w_ref[:, i * step : (i + 2) * step], preferred_element_type=jnp.float32) * weight
        for k in range(2):
            to = slice((i + k) * rows, (i + k + 1) * rows)
            product = wide[:, k * step : (k + 1) * step]
            for c in range(chips):
                mine_ref[c, to, :] = product[8 * c : 8 * c + rows, :].astype(jnp.bfloat16)
                other_ref[c, to, :] = product[8 * (chips + c) : 8 * (chips + c) + rows, :].astype(jnp.bfloat16)


def total_kernel(x_ref, out_ref):
    total = jnp.sum(x_ref[...].astype(jnp.float32), axis=0)
    rows, step = out_ref.shape[0], x_ref.shape[2]
    for i in range(out_ref.shape[1] // step):
        out_ref[:, i * step : (i + 1) * step] = total[i * rows : (i + 1) * rows, :].astype(jnp.bfloat16)


def call(kernel, splits, out_shape, in_specs, scratch, limit, args):
    def body(*refs):
        grouped, at = [], 0
        for size in splits:
            grouped.append(refs[at] if size == 0 else refs[at : at + size])
            at += max(size, 1)
        kernel(*grouped, *refs[at:])

    return pl.pallas_call(
        body,
        out_shape=out_shape,
        in_specs=in_specs,
        out_specs=jax.tree.map(lambda _: VMEM, out_shape),
        scratch_shapes=scratch,
        compiler_params=pltpu.CompilerParams(vmem_limit_bytes=int(limit * 2**20)),
    )(*args)


def on_device(queries, key_rows, value_rows, out_weight, levels, owner_map):
    count = lax.axis_size("seq")
    chips, rows = count // 2, queries.shape[0]
    tokens = rows * count
    heads_dev = out_weight.shape[0] // HD
    width = heads_dev * HD
    keys = key_rows.shape[0]
    extra = -(-2 * heads_dev * tiles_of(tokens, rows) // 8) * 8

    def swap(x, bits):
        return lax.ppermute(x, "seq", [(i, i ^ bits) for i in range(count)])

    there, level_there, owner_there = swap(queries, 1), swap(levels, 1), swap(owner_map, 1)
    key_there, value_there = swap(key_rows, 1), swap(value_rows, 1)
    own = jax.ShapeDtypeStruct((keys, chips * width), key_rows.dtype)
    key_here, value_here = call(
        functools.partial(fetch_kernel, chips),
        (2, 2),
        [own] * 2,
        [IN_HBM] * 2,
        [pltpu.SemaphoreType.DMA((2, chips))],
        FETCH_MIB,
        tuple(pltpu.with_memory_space_constraint(x, pltpu.HBM) for x in (key_rows, value_rows)),
    )
    rest = [key_here, key_there, value_here, value_there]
    rest += [pltpu.with_memory_space_constraint(x, pltpu.HBM) for x in (levels, level_there, owner_map, owner_there)]
    groups = [list(range(c, count, 2)) for c in range(2)]

    def exchange(x):
        return lax.all_to_all(x, "seq", split_axis=0, concat_axis=0, axis_index_groups=groups, tiled=True)

    packed = call(
        functools.partial(pack_kernel, width),
        (),
        jax.ShapeDtypeStruct((GROUPS * 2 * rows, chips * width // GROUPS), jnp.bfloat16),
        [VMEM] * 2,
        [],
        PACK_MIB,
        (pltpu.with_memory_space_constraint(queries, pltpu.HBM), there),
    )
    gathered = [packed] + [swap(packed, 2 * d) for d in range(1, chips)]
    parts = call(
        functools.partial(attend_kernel, tokens, rows, heads_dev),
        (chips, 2, 2, 2, 2, chips),
        [jax.ShapeDtypeStruct((heads_dev * tokens + extra, HD), jnp.bfloat16)] * chips,
        [VMEM] * (chips + 4) + [SMEM] * 4,
        [
            pltpu.VMEM((tokens, chips * width), jnp.bfloat16),
            pltpu.VMEM((tiles_of(tokens, rows) * LANES, LANES), jnp.float32),
        ],
        ATTEND_MIB,
        (*gathered, *rest),
    )
    columns = out_weight.shape[1]
    share = jax.ShapeDtypeStruct((chips, rows * columns // BLOCK, BLOCK), jnp.bfloat16)
    mine, other = call(
        functools.partial(project_kernel, tokens, rows, heads_dev),
        (chips,),
        [share, share],
        [VMEM] * (chips + 1),
        [],
        PROJECT_MIB,
        (parts[0], *(swap(parts[d], 2 * d) for d in range(1, chips)), out_weight),
    )
    summed = exchange((mine.astype(jnp.float32) + swap(other, 1).astype(jnp.float32)).astype(jnp.bfloat16))
    return call(total_kernel, (), jax.ShapeDtypeStruct((rows, columns), jnp.bfloat16), [VMEM], [], 8, (summed,))


def solution(mesh):
    return jax.shard_map(
        on_device,
        mesh=mesh,
        in_specs=(
            P(("groups", "seq"), None),
            P(("groups", "seq"), None),
            P(("groups", "seq"), None),
            P("seq", None),
            P(None, ("groups", "seq")),
            P(None, ("groups", "seq")),
        ),
        out_specs=P(("groups", "seq"), None),
        check_vma=False,
    )
```
